512 devices in a mesh: freq: 32 (over y, z_hi, core), row: 16 (over z_lo, x).
Axes of the slice: x: 4, y: 4, z: 16 (z_hi: 4, z_lo: 4; z = z_hi * 4 + z_lo), core: 2. Of those that a mesh axis runs over, the one named last changes fastest.
Arguments:
- spectral_load: bfloat16 [2, 2048, 4, 600], P(None, 'freq'), may hold values from -6 to 6
- natural_freq: float32 [600], replicated, may hold values from 0.35 to 1.5
- damping: float32 [600], replicated, may hold values from 0.05 to 0.3
- stress_modes: bfloat16 [600, 16384], P(None, 'row'), may hold values from -0.25 to 0.25
- element_volume: float32 [2048], P('row'), may hold values from 0.2 to 2
- row_element: int32 [16384], P('row'), may hold values from 0 to 2047, as said below
- block_case: int32 [64], P('freq'), may hold values from 0 to 3
Outputs:
- grad_loads: float32 [2, 2048, 4, 600], P(None, 'freq')
- grad_damping: float32 [600], replicated
The draws below stay inside these ranges and needn't reach their ends.
Inputs may be any that keep to these rules, and one draw needn't show every extreme that they name: `row_element`: row r belongs to one of the elements (r // 1024) * 128 to (r // 1024 + 1) * 128 - 1.
All inputs are finite; a program needn't handle non-finite values.
Results may differ from the reference program's by a relative error of at most 0.012.
Values may be sent and summed in bfloat16 or wider, within the bound.
A program may use at most 64 MiB of HBM per device.

```python
import math
import jax
import jax.numpy as jnp
from jax import lax

M = 600
NF = 2048
C = 4
TBL = 16
R_DEV = 1024
NT = 1024
NBLK = 64
NROWS = 16384
ELEM_DEV = 128
ELEMS = 2048


def draw_row_element(key, part):
    positions = jnp.arange(NROWS, dtype=jnp.int32)
    offsets = jax.random.randint(key, (NROWS,), 0, ELEM_DEV, dtype=jnp.int32)
    within = positions % R_DEV
    offsets = jnp.where(within == 0, ELEM_DEV - 1, offsets)
    offsets = jnp.where(within == 1, 0, offsets)
    return (positions // R_DEV * ELEM_DEV + offsets).astype(jnp.int32)


def plant(array, stream_key, low, high):
    index_at = [jax.random.randint(jax.random.fold_in(stream_key, axis), (), 0, length) for axis, length in enumerate(array.shape)]
    widest = array.shape.index(max(array.shape))
    beside = index_at[:widest] + [(index_at[widest] + 1) % array.shape[widest]] + index_at[widest + 1:]
    return array.at[tuple(index_at)].set(low).at[tuple(beside)].set(high)


def block_scale(own_key, extent, split, low, largest):
    factor_of = 1.0
    for dim, blocks in split:
        steps = jax.random.uniform(jax.random.fold_in(jax.random.fold_in(own_key, 6), dim), (blocks,), jnp.float32, low / len(split), largest / len(split))
        factor_of = factor_of * jnp.repeat(jnp.exp(steps), extent[dim] // blocks).reshape((-1,) + (1,) * (len(extent) - 1 - dim))
    return factor_of


def bell_draw(stream_key, extent, width, reach, cuts=(), held_as=jnp.bfloat16):
    entries = jax.random.normal(stream_key, extent, jnp.float32) * width
    if len(cuts) > 0:
        entries = block_scale(stream_key, extent, cuts, -0.22, 0.18) * entries
    return jnp.clip(entries, min=-reach, max=reach).astype(held_as)


def setup_inputs(seed: int = 0) -> dict:
    arg_keys = jax.random.split(jax.random.key(seed), 8)
    spectral_load = bell_draw(arg_keys[0], (2, NF, C, M), 1.0, 6.0, ((1, 32),))
    natural_freq = jnp.clip(jnp.exp(jax.random.uniform(arg_keys[1], (M,), jnp.float32, math.log(0.35), math.log(1.5))), 0.35, 1.5)
    damping = jnp.clip(jnp.exp(jax.random.uniform(arg_keys[2], (M,), jnp.float32, math.log(0.05), math.log(0.3))), 0.05, 0.3)
    stress_modes = bell_draw(arg_keys[3], (M, NROWS), M ** -0.5, 0.25, ((1, 16),))
    element_volume = jnp.clip(jnp.exp(math.log(2.0) - 2.3025851 * jax.random.uniform(arg_keys[4], (ELEMS,), jnp.float32) ** block_scale(arg_keys[4], (ELEMS,), ((0, 16),), -0.2, 0.2)), 0.2, 2.0)
    row_element = draw_row_element(jax.random.fold_in(arg_keys[7], 71), 0)
    block_case = plant(jax.random.randint(arg_keys[6], (NBLK,), 0, C), jax.random.fold_in(arg_keys[6], 1), 0, C - 1).astype(jnp.int32)
    return dict(spectral_load=spectral_load, natural_freq=natural_freq, damping=damping, stress_modes=stress_modes, element_volume=element_volume, row_element=row_element, block_case=block_case)


def make_table(freq_index, time_index, line_count):
    product = (freq_index[:, None] * time_index[None, :]) % line_count
    theta = product.astype(jnp.float32) * (2.0 * math.pi / line_count)
    return jnp.stack([jnp.cos(theta), -jnp.sin(theta)]).astype(jnp.bfloat16)


def reference(spectral_load, natural_freq, damping, stress_modes, element_volume, row_element, block_case):
    load = spectral_load.astype(jnp.float32)
    lines = jnp.arange(NF, dtype=jnp.int32)
    omega_f = ((2 * lines + 1).astype(jnp.float32) / NF)[:, None, None]
    omega_m = natural_freq[None, None, :]
    zeta = damping[None, None, :]
    den_real = omega_m * omega_m - omega_f * omega_f
    den_imag = 2.0 * zeta * omega_m * omega_f
    den_abs = den_real * den_real + den_imag * den_imag
    h_real = omega_m * omega_m * den_real / den_abs
    h_imag = -omega_m * omega_m * den_imag / den_abs
    q_real = load[0] * h_real - load[1] * h_imag
    q_imag = load[0] * h_imag + load[1] * h_real
    spectra = jnp.stack([q_real, q_imag]).astype(jnp.bfloat16)
    times = jnp.arange(NT, dtype=jnp.int32)
    table = make_table(lines, times, NF).astype(jnp.float32)
    factor = float(NF) ** -0.5
    history = jnp.einsum("kfn,kfcm->ncm", table, spectra.astype(jnp.float32), precision=lax.Precision.HIGHEST) * factor
    case_time = jnp.repeat(block_case, TBL)
    selector = (case_time[:, None] == jnp.arange(C, dtype=jnp.int32)[None, :]).astype(jnp.float32)
    usel = jnp.sum(history * selector[:, :, None], axis=1).astype(jnp.bfloat16)
    stress = jnp.dot(usel, stress_modes, preferred_element_type=jnp.float32)
    weight = element_volume[row_element]
    scale = float(M * NF) / float(NROWS * NT)
    gstress = (2.0 * scale * weight[None, :] * stress).astype(jnp.bfloat16)
    gusel = jnp.dot(gstress, stress_modes.T, preferred_element_type=jnp.float32).astype(jnp.bfloat16)
    gu = (gusel.astype(jnp.float32)[:, None, :] * selector[:, :, None]).astype(jnp.bfloat16)
    gq = jnp.einsum("kfn,ncm->kfcm", table, gu.astype(jnp.float32), precision=lax.Precision.HIGHEST) * factor
    grad_real = gq[0] * h_real + gq[1] * h_imag
    grad_imag = -gq[0] * h_imag + gq[1] * h_real
    grad_loads = jnp.stack([grad_real, grad_imag])
    ratio = omega_f / omega_m
    p_real = q_real * h_real - q_imag * h_imag
    p_imag = q_real * h_imag + q_imag * h_real
    grad_damping = jnp.sum(2.0 * ratio * (gq[0] * p_imag - gq[1] * p_real), axis=(0, 1))
    return grad_loads, grad_damping
```

```python
import functools
import itertools
import math

import jax
import jax.numpy as jnp
from jax import lax
from jax.experimental import pallas as pl
from jax.experimental.pallas import tpu as pltpu
from jax.sharding import PartitionSpec as P

TBL = 16
MESH = pl.DeviceIdType.MESH
F32 = jnp.float32
BF16 = jnp.bfloat16
SIZES = dict(y=4, zh=4, c=2, zl=4, x=4)


def offsets(*axes):
    steps = itertools.product(*[range(SIZES[a]) for a in axes])
    return [dict(zip(axes, s)) for s in steps if any(s)]


YC = offsets("y", "c")
ZH = offsets("zh")
ZL = offsets("zl")
X = offsets("x")
XY = offsets("x", "y")
PEERS = YC + ZH + ZL + [o for o in XY if o["x"]]


def cosine(index):
    t = (jnp.abs(index - 1024) - 512).astype(F32) * (math.pi / 1024)
    s = t * t
    poly = -1.0 / 39916800
    for term in (1.0 / 362880, -1.0 / 5040, 1.0 / 120, -1.0 / 6, 1.0):
        poly = poly * s + term
    return t * poly


def kernel(
    lines, scale, load_hbm, nf_ref, dm_ref, modes_hbm, ev_ref, re_ref, bc_ref, out_ref, gd_ref,
    load, stress, spec, zspec, snd, prcv, cbuf, ksnd, kx, kz, kbuf, p2, lbuf, gbuf, dbuf, dcore, tab, hr_ref, hi_ref,
    load_sem, stress_sem, c1s, c1r, c2s, c2r, p1s, p1r, kxs, kxr, kzs, kzr, kas, kar, kcs, kcr,
    p2s, p2r, ls, lr, gs, gr, ds, dr, gcs, gcr, dcs, dcr,
):
    fpos = lax.axis_index("freq")
    rpos = lax.axis_index("row")
    me = dict(y=fpos // 8, zh=lax.rem(fpos // 2, 4), c=lax.rem(fpos, 2), zl=rpos // 4, x=lax.rem(rpos, 4))
    y, zh, c, zl, x = me["y"], me["zh"], me["c"], me["zl"], me["x"]
    yc = 2 * y + c

    def at(off):
        return {k: lax.rem(me[k] + off[k], SIZES[k]) if off.get(k) else me[k] for k in SIZES}

    def dev(off):
        o = at(off)
        return {"freq": o["y"] * 8 + o["zh"] * 2 + o["c"], "row": o["zl"] * 4 + o["x"]}

    def send(src, dst, ssem, rsem, off):
        copy = pltpu.make_async_remote_copy(
            src_ref=src, dst_ref=dst, send_sem=ssem, recv_sem=rsem, device_id=dev(off), device_id_type=MESH
        )
        copy.start()
        return copy

    barrier = pltpu.get_barrier_semaphore()
    for off in PEERS:
        pl.semaphore_signal(barrier, inc=1, device_id=dev(off), device_id_type=MESH)
    modes = nf_ref.shape[1]
    cp_stress = pltpu.make_async_copy(modes_hbm, stress.at[pl.ds(0, modes)], stress_sem)
    cp_stress.start()
    cp_load = pltpu.make_async_copy(load_hbm, load, load_sem)
    cp_load.start()

    elem = re_ref[...] - rpos * ev_ref.shape[1]
    eye = lax.broadcasted_iota(jnp.int32, (128, 128), 0) == lax.broadcasted_iota(jnp.int32, (128, 128), 1)
    vol = jnp.sum(jnp.where(eye, jnp.broadcast_to(ev_ref[...], (128, 128)), 0.0), axis=1, keepdims=True)
    onehot = lax.broadcasted_iota(jnp.int32, (128, elem.shape[1]), 0) == elem
    weight = jnp.sum(jnp.where(onehot, vol, 0.0), axis=0, keepdims=True) * (2.0 * scale)

    row = lax.broadcasted_iota(jnp.int32, (64, 512), 0)
    lane = lax.broadcasted_iota(jnp.int32, (64, 512), 1)
    ph = jnp.bitwise_and((64 * fpos + (lane % 256) // 4) * (64 * rpos + row) + 512 * (lane // 256), 2047)
    fwd = cosine(ph).reshape(8, 1, 8, 512)
    fwd = jnp.broadcast_to(fwd, (8, 4, 8, 512)).reshape(256, 512)
    row = lax.broadcasted_iota(jnp.int32, (256, 512), 0)
    lane = lax.broadcasted_iota(jnp.int32, (256, 512), 1)
    fwd = jnp.where((row // 8) % 4 == lane % 4, fwd, 0.0).astype(BF16)

    cp_stress.wait()
    stress[pl.ds(modes, 768 - modes), :] = jnp.zeros((768 - modes, stress.shape[1]), BF16)
    part = stress[pl.ds(pl.multiple_of(96 * yc, 32), 96), :].astype(F32) * weight
    kpart = lax.dot_general(
        part.astype(BF16), stress[pl.ds(0, modes), :], (((1,), (1,)), ((), ())), preferred_element_type=F32
    )
    ksnd[...] = kpart.reshape(4, 3, 8, modes).astype(BF16)
    kx[x] = ksnd[x]

    cp_load.wait()
    row = lax.broadcasted_iota(jnp.int32, (256, modes), 0)
    wf = (2 * (64 * fpos + row // 4) + 1).astype(F32) * (1.0 / lines)
    wm = nf_ref[...]
    wm2 = wm * wm
    den_real = wm2 - wf * wf
    den_imag = 2.0 * dm_ref[...] * wm * wf
    gain = wm2 / (den_real * den_real + den_imag * den_imag)
    h_real = gain * den_real
    h_imag = -gain * den_imag
    hr_ref[...] = h_real
    hi_ref[...] = h_imag
    l_real = load[0].astype(F32).reshape(256, modes)
    l_imag = load[1].astype(F32).reshape(256, modes)
    q_real = l_real * h_real - l_imag * h_imag
    q_imag = l_real * h_imag + l_imag * h_real
    spec[pl.ds(0, 256), :] = q_real.astype(BF16)
    spec[pl.ds(256, 256), :] = q_imag.astype(BF16)
    ratio = 2.0 * wf / wm
    zspec[pl.ds(0, 256), :] = (ratio * (q_real * h_imag + q_imag * h_real)).astype(BF16)
    zspec[pl.ds(256, 256), :] = (ratio * (q_imag * h_imag - q_real * h_real)).astype(BF16)
    snd[:, pl.ds(0, 32), :] = jnp.dot(fwd, spec[...], preferred_element_type=F32).astype(BF16).reshape(8, 32, modes)
    snd[:, pl.ds(32, 32), :] = jnp.dot(fwd, zspec[...], preferred_element_type=F32).astype(BF16).reshape(8, 32, modes)
    prcv[yc] = snd[yc]
    for b in range(2):
        cbuf[zh, yc, pl.ds(b, 1), :] = jnp.full((1, 128), bc_ref[b], jnp.int32).astype(F32)

    pl.semaphore_wait(barrier, len(PEERS))
    copies = []
    c1 = [send(cbuf.at[zh, yc], cbuf.at[zh, yc], c1s.at[i], c1r.at[i], o) for i, o in enumerate(YC)]
    p1 = []
    for i, o in enumerate(YC):
        t = at(o)
        p1.append(send(snd.at[2 * t["y"] + t["c"]], prcv.at[yc], p1s.at[i], p1r.at[i], o))
    kxc = [send(ksnd.at[at(o)["x"]], kx.at[x], kxs.at[i], kxr.at[i], o) for i, o in enumerate(X)]
    for cp in c1:
        cp.wait_recv()
    c2 = [send(cbuf.at[zh], cbuf.at[zh], c2s.at[i], c2r.at[i], o) for i, o in enumerate(ZH)]

    for cp in kxc:
        cp.wait_recv()
    kz[zl] = jnp.sum(kx[...].astype(F32), axis=0).astype(BF16)
    kzc = [send(kz.at[zl], kz.at[zl], kzs.at[i], kzr.at[i], o) for i, o in enumerate(ZL)]
    for cp in kzc:
        cp.wait_recv()
    kbuf[y, c, x] = jnp.sum(kz[...].astype(F32), axis=0).astype(BF16)
    kac = [send(kbuf.at[y, c, x], kbuf.at[y, c, x], kas.at[i], kar.at[i], o) for i, o in enumerate(XY)]

    for cp in p1:
        cp.wait_recv()
    tot = prcv[0].astype(F32)
    for q in range(1, 8):
        tot += prcv[q].astype(F32)
    for cp in c2:
        cp.wait_recv()
    both = cbuf[x, 2 * zl + y // 2]
    case = jnp.where(lax.rem(y, 2) == 0, both[0:1, 0:1], both[1:2, 0:1])
    usel = jnp.zeros((8, modes), F32)
    vsel = jnp.zeros((8, modes), F32)
    for k in range(4):
        usel = jnp.where(case == k, tot[8 * k:8 * k + 8], usel)
        vsel = jnp.where(case == k, tot[32 + 8 * k:40 + 8 * k], vsel)
    p2[zh] = jnp.concatenate([usel, vsel], axis=0).astype(BF16)
    p2c = [send(p2.at[zh], p2.at[zh], p2s.at[i], p2r.at[i], o) for i, o in enumerate(ZH)]

    spread = (
        lax.broadcasted_iota(jnp.int32, (512, 128), 0) // 4 == lax.broadcasted_iota(jnp.int32, (512, 128), 1)
    ).astype(BF16)
    rcase = (lax.broadcasted_iota(jnp.int32, (512, 128), 0) % 4).astype(F32)
    trow = lax.broadcasted_iota(jnp.int32, (128, 128), 0)
    tlane = lax.broadcasted_iota(jnp.int32, (128, 128), 1)
    clane = lax.broadcasted_iota(jnp.int32, (1, 128), 1)
    for xs in range(4):
        cases = jnp.zeros((1, 128), F32)
        for ys in range(4):
            for zs in range(4):
                mine = jnp.logical_and(clane // 32 == ys, (clane // 8) % 4 == zs)
                cases = jnp.where(mine, cbuf[xs, 2 * zs + ys // 2, pl.ds(ys % 2, 1), :], cases)
        keep = rcase == cases
        for cs in range(2):
            n = 64 * (4 * ((tlane // 8) % 4) + xs) + 8 * (2 * (tlane // 32) + cs) + tlane % 8
            ph = jnp.bitwise_and((64 * fpos + trow % 64) * n + 512 * (trow // 64), 2047)
            wide = jnp.dot(spread, cosine(ph).astype(BF16), preferred_element_type=F32)
            tab[:, pl.ds(512 * cs + 128 * xs, 128)] = jnp.where(keep, wide, 0.0).astype(BF16)

    for cp in kac:
        cp.wait_recv()
    kcc = send(kbuf.at[:, c], kbuf.at[:, c], kcs, kcr, dict(c=1))
    kcc.wait_recv()
    for cp in p2c:
        cp.wait_recv()
    factor = float(lines) ** -0.5
    tot = jnp.sum(p2[...].astype(F32), axis=0) * factor
    kmat = kbuf[...].reshape(32, 24, modes)[0:25].reshape(600, modes)
    g = jnp.dot(tot[0:8].astype(BF16), kmat, preferred_element_type=F32)
    g = g.astype(BF16).astype(F32)
    d = jnp.sum(g * tot[8:16], axis=0, keepdims=True)
    d_hi = d.astype(BF16).astype(F32)
    lbuf[zl] = jnp.concatenate([g, d_hi, d - d_hi, jnp.zeros((6, modes), F32)], axis=0).astype(BF16)
    lc = [send(lbuf.at[zl], lbuf.at[zl], ls.at[i], lr.at[i], o) for i, o in enumerate(ZL)]
    for cp in lc:
        cp.wait_recv()
    got = lbuf[...].astype(F32)
    slot = 4 * x + y
    gbuf[c, slot] = got[:, 0:8].reshape(32, modes).astype(BF16)
    dbuf[slot] = jnp.sum(got[:, 8:10], axis=(0, 1), keepdims=True).reshape(1, modes)
    gc = [send(gbuf.at[c, slot], gbuf.at[c, slot], gs.at[i], gr.at[i], o) for i, o in enumerate(XY)]
    dc = [send(dbuf.at[slot], dbuf.at[slot], ds.at[i], dr.at[i], o) for i, o in enumerate(XY)]
    fc = [send(gbuf.at[c, slot], gbuf.at[c, slot], gcs.at[15], gcr.at[15], dict(c=1))]
    for i, o in enumerate(XY):
        gc[i].wait_recv()
        b = 4 * lax.rem(x + 4 - o["x"], 4) + lax.rem(y + 4 - o["y"], 4)
        fc.append(send(gbuf.at[c, b], gbuf.at[c, b], gcs.at[i], gcr.at[i], dict(c=1)))
    for cp in dc:
        cp.wait_recv()
    dcore[c] = jnp.sum(dbuf[...], axis=0)
    dcc = send(dcore.at[c], dcore.at[c], dcs, dcr, dict(c=1))
    for cp in fc:
        cp.wait_recv()
    gq = jnp.dot(tab[...], gbuf[...].reshape(1024, modes), preferred_element_type=F32) * factor
    h_real = hr_ref[...]
    h_imag = hi_ref[...]
    out_ref[0] = (gq[0:256] * h_real + gq[256:512] * h_imag).reshape(64, 4, modes)
    out_ref[1] = (gq[256:512] * h_real - gq[0:256] * h_imag).reshape(64, 4, modes)
    dcc.wait_recv()
    gd_ref[...] = dcore[0] + dcore[1]
    for cp in c1 + c2 + p1 + kxc + kzc + kac + [kcc] + p2c + lc + gc + dc + fc + [dcc]:
        cp.wait_send()


def per_device(spectral_load, natural_freq, damping, stress_modes, element_volume, row_element, block_case):
    _, freq_dev, cases, modes = spectral_load.shape
    lines = freq_dev * lax.axis_size("freq")
    rows = stress_modes.shape[1]
    times = block_case.shape[0] * TBL * lax.axis_size("freq")
    scale = float(modes * lines) / float(rows * lax.axis_size("row") * times)
    vmem = pl.BlockSpec(memory_space=pltpu.VMEM)
    dma = pltpu.SemaphoreType.DMA
    sems = [None, None, 7, 7, 3, 3, 7, 7, 3, 3, 3, 3, 15, 15, None, None, 3, 3, 3, 3, 15, 15, 15, 15, 16, 16, None, None]
    out, gd = pl.pallas_call(
        functools.partial(kernel, lines, scale),
        out_shape=(
            jax.ShapeDtypeStruct((2, freq_dev, cases, modes), F32),
            jax.ShapeDtypeStruct((1, modes), F32),
        ),
        in_specs=[
            pl.BlockSpec(memory_space=pl.ANY), vmem, vmem, pl.BlockSpec(memory_space=pl.ANY), vmem, vmem,
            pl.BlockSpec(memory_space=pltpu.SMEM),
        ],
        out_specs=(vmem, vmem),
        scratch_shapes=[
            pltpu.VMEM((2, freq_dev, cases, modes), BF16),
            pltpu.VMEM((768, rows), BF16),
            pltpu.VMEM((512, modes), BF16),
            pltpu.VMEM((512, modes), BF16),
            pltpu.VMEM((8, 64, modes), BF16),
            pltpu.VMEM((8, 64, modes), BF16),
            pltpu.VMEM((4, 8, 2, 128), F32),
            pltpu.VMEM((4, 3, 8, modes), BF16),
            pltpu.VMEM((4, 3, 8, modes), BF16),
            pltpu.VMEM((4, 3, 8, modes), BF16),
            pltpu.VMEM((4, 2, 4, 3, 8, modes), BF16),
            pltpu.VMEM((4, 16, modes), BF16),
            pltpu.VMEM((4, 16, modes), BF16),
            pltpu.VMEM((2, 16, 32, modes), BF16),
            pltpu.VMEM((16, 1, modes), F32),
            pltpu.VMEM((2, 1, modes), F32),
            pltpu.VMEM((512, 1024), BF16),
            pltpu.VMEM((256, modes), F32),
            pltpu.VMEM((256, modes), F32),
        ] + [dma if s is None else dma((s,)) for s in sems],
        compiler_params=pltpu.CompilerParams(
            collective_id=0, has_side_effects=True, vmem_limit_bytes=48 * 1024 * 1024
        ),
        name="adjoint",
    )(
        spectral_load,
        natural_freq.reshape(1, modes),
        damping.reshape(1, modes),
        stress_modes,
        element_volume.reshape(1, -1),
        row_element.reshape(1, rows),
        block_case,
    )
    return out, gd.reshape(modes)


def solution(mesh):
    return jax.shard_map(
        per_device,
        mesh=mesh,
        in_specs=(
            P(None, "freq", None, None),
            P(),
            P(),
            P(None, "row"),
            P("row"),
            P("row"),
            P("freq"),
        ),
        out_specs=(P(None, "freq", None, None), P()),
        check_vma=False,
    )
```

```python
import functools
import itertools
import math

import jax
import jax.numpy as jnp
from jax import lax
from jax.experimental import pallas as pl
from jax.experimental.pallas import tpu as pltpu
from jax.sharding import PartitionSpec as P

TBL = 16
MESH = pl.DeviceIdType.MESH
F32 = jnp.float32
BF16 = jnp.bfloat16
SIZES = dict(y=4, zh=4, c=2, zl=4, x=4)


def offsets(*axes):
    steps = itertools.product(*[range(SIZES[a]) for a in axes])
    return [dict(zip(axes, s)) for s in steps if any(s)]


YC = offsets("y", "c")
ZH = offsets("zh")
ZL = offsets("zl")
X = offsets("x")
XY = offsets("x", "y")
PEERS = YC + ZH + ZL + [o for o in XY if o["x"]]


def cosine(index):
    t = (jnp.abs(index - 1024) - 512).astype(F32) * (math.pi / 1024)
    s = t * t
    poly = -1.0 / 39916800
    for term in (1.0 / 362880, -1.0 / 5040, 1.0 / 120, -1.0 / 6, 1.0):
        poly = poly * s + term
    return t * poly


def kernel(
    lines, scale, load_hbm, nf_hbm, dm_hbm, modes_hbm, ev_hbm, re_hbm, bc_hbm, out_ref, gd_ref,
    load, nf, dm, stress, ev, re, bc, spec, zspec, usnd, vsnd, urcv, vrcv, own, cbuf, ksnd, kx, kz, kbuf, pu, pv,
    lbuf, dl, gbuf, dbuf, dcore, tab, hr_ref, hi_ref,
    in_sem, os, orr, c1s, c1r, c2s, c2r, p1s, p1r, v1s, v1r, kxs, kxr, kzs, kzr, kas, kar, kcs, kcr,
    p2s, p2r, v2s, v2r, ls, lr, dls, dlr, gs, gr, ds, dr, gcs, gcr, dcs, dcr,
):
    fpos = lax.axis_index("freq")
    rpos = lax.axis_index("row")
    me = dict(y=fpos // 8, zh=lax.rem(fpos // 2, 4), c=lax.rem(fpos, 2), zl=rpos // 4, x=lax.rem(rpos, 4))
    y, zh, c, zl, x = me["y"], me["zh"], me["c"], me["zl"], me["x"]
    yc = 2 * y + c
    sent = []

    def at(off):
        return {k: lax.rem(me[k] + off[k], SIZES[k]) if off.get(k) else me[k] for k in SIZES}

    def ident(o):
        return {"freq": o["y"] * 8 + o["zh"] * 2 + o["c"], "row": o["zl"] * 4 + o["x"]}

    def copy_to(src, dst, ssem, rsem, device):
        return pltpu.make_async_remote_copy(
            src_ref=src, dst_ref=dst, send_sem=ssem, recv_sem=rsem, device_id=device, device_id_type=MESH
        )

    def send(src, dst, ssem, rsem, off):
        copy = copy_to(src, dst, ssem, rsem, ident(at(off)))
        copy.start()
        sent.append(copy)
        return copy

    def arrive(copies):
        for copy in copies:
            copy.wait_recv()

    owner = {"freq": zl * 8 + x * 2 + y // 2, "row": rpos}
    orphan = fpos != owner["freq"]
    serves = jnp.logical_and(y == zl, zh == x)
    wards = jnp.where(serves, jnp.where(y // 2 == c, 15, 16), 0)

    barrier = pltpu.get_barrier_semaphore()
    for off in ZH + ZL + YC + [o for o in XY if o["x"]]:
        pl.semaphore_signal(barrier, inc=1, device_id=ident(at(off)), device_id_type=MESH)

    @pl.when(orphan)
    def _():
        pl.semaphore_signal(barrier, inc=1, device_id=owner, device_id_type=MESH)

    modes = nf.shape[0]
    local = [
        pltpu.make_async_copy(src, dst, in_sem.at[i])
        for i, (src, dst) in enumerate([
            (re_hbm, re), (ev_hbm, ev), (modes_hbm, stress.at[pl.ds(0, modes)]),
            (nf_hbm, nf), (dm_hbm, dm), (bc_hbm, bc), (load_hbm, load),
        ])
    ]
    for cp in local:
        cp.start()

    row = lax.broadcasted_iota(jnp.int32, (64, 512), 0)
    lane = lax.broadcasted_iota(jnp.int32, (64, 512), 1)
    ph = jnp.bitwise_and((64 * fpos + (lane % 256) // 4) * (64 * rpos + row) + 512 * (lane // 256), 2047)
    fwd = cosine(ph).reshape(8, 1, 8, 512)
    fwd = jnp.broadcast_to(fwd, (8, 4, 8, 512)).reshape(256, 512)
    row = lax.broadcasted_iota(jnp.int32, (256, 512), 0)
    lane = lax.broadcasted_iota(jnp.int32, (256, 512), 1)
    fwd = jnp.where((row // 8) % 4 == lane % 4, fwd, 0.0).astype(BF16)

    for cp in local[3:]:
        cp.wait()
    row = lax.broadcasted_iota(jnp.int32, (256, modes), 0)
    wf = (2 * (64 * fpos + row // 4) + 1).astype(F32) * (1.0 / lines)
    wm = nf[...].reshape(1, modes)
    wm2 = wm * wm
    den_real = wm2 - wf * wf
    den_imag = 2.0 * dm[...].reshape(1, modes) * wm * wf
    gain = wm2 / (den_real * den_real + den_imag * den_imag)
    h_real = gain * den_real
    h_imag = -gain * den_imag
    hr_ref[...] = h_real
    hi_ref[...] = h_imag
    l_real = load[0].astype(F32).reshape(256, modes)
    l_imag = load[1].astype(F32).reshape(256, modes)
    q_real = l_real * h_real - l_imag * h_imag
    q_imag = l_real * h_imag + l_imag * h_real
    spec[pl.ds(0, 256), :] = q_real.astype(BF16)
    spec[pl.ds(256, 256), :] = q_imag.astype(BF16)
    ratio = 2.0 * wf / wm
    zspec[pl.ds(0, 256), :] = (ratio * (q_real * h_imag + q_imag * h_real)).astype(BF16)
    zspec[pl.ds(256, 256), :] = (ratio * (q_imag * h_imag - q_real * h_real)).astype(BF16)
    usnd[...] = jnp.dot(fwd, spec[...], preferred_element_type=F32).astype(BF16).reshape(8, 32, modes)
    vsnd[...] = jnp.dot(fwd, zspec[...], preferred_element_type=F32).astype(BF16).reshape(8, 32, modes)
    urcv[yc] = usnd[yc]
    vrcv[yc] = vsnd[yc]
    for b in range(2):
        cbuf[zh, yc, pl.ds(b, 1), :] = jnp.full((1, 128), bc[b], jnp.int32).astype(F32)

    for cp in local[:3]:
        cp.wait()
    elem = re[...].reshape(1, re.shape[0]) - rpos * ev.shape[0]
    eye = lax.broadcasted_iota(jnp.int32, (128, 128), 0) == lax.broadcasted_iota(jnp.int32, (128, 128), 1)
    vol = jnp.broadcast_to(ev[...].reshape(1, 128), (128, 128))
    vol = jnp.sum(jnp.where(eye, vol, 0.0), axis=1, keepdims=True)
    onehot = lax.broadcasted_iota(jnp.int32, (128, elem.shape[1]), 0) == elem
    weight = jnp.sum(jnp.where(onehot, vol, 0.0), axis=0, keepdims=True) * (2.0 * scale)
    stress[pl.ds(modes, 768 - modes), :] = jnp.zeros((768 - modes, stress.shape[1]), BF16)
    part = stress[pl.ds(pl.multiple_of(96 * yc, 32), 96), :].astype(F32) * weight
    kpart = lax.dot_general(
        part.astype(BF16), stress[pl.ds(0, modes), :], (((1,), (1,)), ((), ())), preferred_element_type=F32
    )
    ksnd[...] = kpart.reshape(4, 3, 8, modes).astype(BF16)
    kx[x] = ksnd[x]

    pl.semaphore_wait(barrier, len(PEERS) + wards)

    served = []
    for i, (dy, z, e) in enumerate(itertools.product(range(2), range(4), range(2))):
        target = (2 * c + dy) * 8 + z * 2 + e
        served.append((target, copy_to(cbuf.at[zh, yc], own, os.at[i], orr, {"freq": target, "row": rpos})))

    @pl.when(serves)
    def _():
        for target, cp in served:
            @pl.when(target != fpos)
            def _(cp=cp):
                cp.start()

    p1 = []
    for i, o in enumerate(YC):
        t = at(o)
        p1.append(send(usnd.at[2 * t["y"] + t["c"]], urcv.at[yc], p1s.at[i], p1r.at[i], o))
    c1 = [send(cbuf.at[zh, yc], cbuf.at[zh, yc], c1s.at[i], c1r.at[i], o) for i, o in enumerate(YC)]
    kxc = [send(ksnd.at[at(o)["x"]], kx.at[x], kxs.at[i], kxr.at[i], o) for i, o in enumerate(X)]
    v1 = []
    for i, o in enumerate(YC):
        t = at(o)
        v1.append(send(vsnd.at[2 * t["y"] + t["c"]], vrcv.at[yc], v1s.at[i], v1r.at[i], o))

    arrive(kxc)
    kz[zl] = jnp.sum(kx[...].astype(F32), axis=0).astype(BF16)
    kzc = [send(kz.at[zl], kz.at[zl], kzs.at[i], kzr.at[i], o) for i, o in enumerate(ZL)]

    arrive(p1)
    usum = jnp.sum(urcv[...].astype(F32), axis=0)

    @pl.when(orphan)
    def _():
        copy_to(cbuf.at[zh, yc], own, os.at[0], orr, owner).wait_recv()

    @pl.when(jnp.logical_not(orphan))
    def _():
        own[...] = cbuf[zh, yc]

    case = jnp.where(lax.rem(y, 2) == 0, own[0:1, 0:1], own[1:2, 0:1])

    def pick(rows):
        sel = jnp.zeros((8, modes), F32)
        for k in range(4):
            sel = jnp.where(case == k, rows[8 * k:8 * k + 8], sel)
        return sel.astype(BF16)

    pu[zh] = pick(usum)
    p2 = [send(pu.at[zh], pu.at[zh], p2s.at[i], p2r.at[i], o) for i, o in enumerate(ZH)]
    arrive(v1)
    pv[zh] = pick(jnp.sum(vrcv[...].astype(F32), axis=0))
    v2 = [send(pv.at[zh], pv.at[zh], v2s.at[i], v2r.at[i], o) for i, o in enumerate(ZH)]
    arrive(c1)
    c2 = [send(cbuf.at[zh], cbuf.at[zh], c2s.at[i], c2r.at[i], o) for i, o in enumerate(ZH)]
    arrive(kzc)
    kbuf[y, c, x] = jnp.sum(kz[...].astype(F32), axis=0).astype(BF16)
    kac = [send(kbuf.at[y, c, x], kbuf.at[y, c, x], kas.at[i], kar.at[i], o) for i, o in enumerate(XY)]
    arrive(kac)
    kcc = send(kbuf.at[:, c], kbuf.at[:, c], kcs, kcr, dict(c=1))
    arrive([kcc])
    arrive(p2)
    factor = float(lines) ** -0.5
    usel = (jnp.sum(pu[...].astype(F32), axis=0) * factor).astype(BF16)
    kmat = kbuf[...].reshape(32, 24, modes)[0:25].reshape(600, modes)
    g = jnp.dot(usel, kmat, preferred_element_type=F32).astype(BF16)
    lbuf[zl] = g
    lc = [send(lbuf.at[zl], lbuf.at[zl], ls.at[i], lr.at[i], o) for i, o in enumerate(ZL)]
    arrive(v2)
    vsel = jnp.sum(pv[...].astype(F32), axis=0) * factor
    dl[zl] = jnp.sum(g.astype(F32) * vsel, axis=0, keepdims=True)
    dlc = [send(dl.at[zl], dl.at[zl], dls.at[i], dlr.at[i], o) for i, o in enumerate(ZL)]
    arrive(lc)
    slot = 4 * x + y
    gbuf[c, slot] = lbuf[...].astype(F32).reshape(32, modes).astype(BF16)
    gc = [send(gbuf.at[c, slot], gbuf.at[c, slot], gs.at[i], gr.at[i], o) for i, o in enumerate(XY)]
    fc = [send(gbuf.at[c, slot], gbuf.at[c, slot], gcs.at[15], gcr.at[15], dict(c=1))]
    arrive(dlc)
    dbuf[slot] = jnp.sum(dl[...], axis=0)
    dc = [send(dbuf.at[slot], dbuf.at[slot], ds.at[i], dr.at[i], o) for i, o in enumerate(XY)]

    arrive(c2)
    spread = (
        lax.broadcasted_iota(jnp.int32, (512, 128), 0) // 4 == lax.broadcasted_iota(jnp.int32, (512, 128), 1)
    ).astype(BF16)
    rcase = (lax.broadcasted_iota(jnp.int32, (512, 128), 0) % 4).astype(F32)
    trow = lax.broadcasted_iota(jnp.int32, (128, 128), 0)
    tlane = lax.broadcasted_iota(jnp.int32, (128, 128), 1)
    clane = lax.broadcasted_iota(jnp.int32, (1, 128), 1)
    for xs in range(4):
        cases = jnp.zeros((1, 128), F32)
        for ys in range(4):
            for zs in range(4):
                mine = jnp.logical_and(clane // 32 == ys, (clane // 8) % 4 == zs)
                cases = jnp.where(mine, cbuf[xs, 2 * zs + ys // 2, pl.ds(ys % 2, 1), :], cases)
        keep = rcase == cases
        for cs in range(2):
            n = 64 * (4 * ((tlane // 8) % 4) + xs) + 8 * (2 * (tlane // 32) + cs) + tlane % 8
            ph = jnp.bitwise_and((64 * fpos + trow % 64) * n + 512 * (trow // 64), 2047)
            wide = jnp.dot(spread, cosine(ph).astype(BF16), preferred_element_type=F32)
            tab[cs, :, pl.ds(128 * xs, 128)] = jnp.where(keep, wide, 0.0).astype(BF16)

    for i, o in enumerate(XY):
        arrive([gc[i]])
        b = 4 * lax.rem(x + 4 - o["x"], 4) + lax.rem(y + 4 - o["y"], 4)
        fc.append(send(gbuf.at[c, b], gbuf.at[c, b], gcs.at[i], gcr.at[i], dict(c=1)))
    gq = jnp.dot(tab[c], gbuf[c].reshape(512, modes), preferred_element_type=F32)
    arrive(dc)
    dcore[c] = jnp.sum(dbuf[...], axis=0)
    dcc = send(dcore.at[c], dcore.at[c], dcs, dcr, dict(c=1))
    arrive(fc)
    gq = (gq + jnp.dot(tab[1 - c], gbuf[1 - c].reshape(512, modes), preferred_element_type=F32)) * factor
    h_real = hr_ref[...]
    h_imag = hi_ref[...]
    out_ref[0] = (gq[0:256] * h_real + gq[256:512] * h_imag).reshape(64, 4, modes)
    out_ref[1] = (gq[256:512] * h_real - gq[0:256] * h_imag).reshape(64, 4, modes)
    arrive([dcc])
    gd_ref[...] = (dcore[0] + dcore[1]).reshape(modes)

    @pl.when(serves)
    def _():
        for target, cp in served:
            @pl.when(target != fpos)
            def _(cp=cp):
                cp.wait_send()

    for cp in sent:
        cp.wait_send()


def per_device(spectral_load, natural_freq, damping, stress_modes, element_volume, row_element, block_case):
    _, freq_dev, cases, modes = spectral_load.shape
    lines = freq_dev * lax.axis_size("freq")
    rows = stress_modes.shape[1]
    times = block_case.shape[0] * TBL * lax.axis_size("freq")
    scale = float(modes * lines) / float(rows * lax.axis_size("row") * times)
    hbm = pl.BlockSpec(memory_space=pltpu.HBM)
    vmem = pl.BlockSpec(memory_space=pltpu.VMEM)
    dma = pltpu.SemaphoreType.DMA
    pairs = [7, 3, 7, 7, 3, 3, 15, None, 3, 3, 3, 3, 15, 15, 16, None]
    return pl.pallas_call(
        functools.partial(kernel, lines, scale),
        out_shape=(
            jax.ShapeDtypeStruct((2, freq_dev, cases, modes), F32),
            jax.ShapeDtypeStruct((modes,), F32),
        ),
        in_specs=[hbm] * 7,
        out_specs=(vmem, vmem),
        scratch_shapes=[
            pltpu.VMEM((2, freq_dev, cases, modes), BF16),
            pltpu.VMEM((modes,), F32),
            pltpu.VMEM((modes,), F32),
            pltpu.VMEM((768, rows), BF16),
            pltpu.VMEM(element_volume.shape, F32),
            pltpu.VMEM(row_element.shape, jnp.int32),
            pltpu.SMEM(block_case.shape, jnp.int32),
            pltpu.VMEM((512, modes), BF16),
            pltpu.VMEM((512, modes), BF16),
            pltpu.VMEM((8, 32, modes), BF16),
            pltpu.VMEM((8, 32, modes), BF16),
            pltpu.VMEM((8, 32, modes), BF16),
            pltpu.VMEM((8, 32, modes), BF16),
            pltpu.VMEM((2, 128), F32),
            pltpu.VMEM((4, 8, 2, 128), F32),
            pltpu.VMEM((4, 3, 8, modes), BF16),
            pltpu.VMEM((4, 3, 8, modes), BF16),
            pltpu.VMEM((4, 3, 8, modes), BF16),
            pltpu.VMEM((4, 2, 4, 3, 8, modes), BF16),
            pltpu.VMEM((4, 8, modes), BF16),
            pltpu.VMEM((4, 8, modes), BF16),
            pltpu.VMEM((4, 8, modes), BF16),
            pltpu.VMEM((4, 1, modes), F32),
            pltpu.VMEM((2, 16, 32, modes), BF16),
            pltpu.VMEM((16, 1, modes), F32),
            pltpu.VMEM((2, 1, modes), F32),
            pltpu.VMEM((2, 512, 512), BF16),
            pltpu.VMEM((256, modes), F32),
            pltpu.VMEM((256, modes), F32),
            dma((7,)), dma((16,)), dma,
        ] + [dma if s is None else dma((s,)) for s in pairs for _ in range(2)],
        compiler_params=pltpu.CompilerParams(
            collective_id=0, has_side_effects=True, vmem_limit_bytes=56 * 1024 * 1024
        ),
        name="adjoint",
    )(spectral_load, natural_freq, damping, stress_modes, element_volume, row_element, block_case)


def solution(mesh):
    return jax.shard_map(
        per_device,
        mesh=mesh,
        in_specs=(
            P(None, "freq", None, None),
            P(),
            P(),
            P(None, "row"),
            P("row"),
            P("row"),
            P("freq"),
        ),
        out_specs=(P(None, "freq", None, None), P()),
        check_vma=False,
    )
```

```python
import functools
import itertools
import math

import jax
import jax.numpy as jnp
from jax import lax
from jax.experimental import pallas as pl
from jax.experimental.pallas import tpu as pltpu
from jax.sharding import PartitionSpec as P

TBL = 16
MESH = pl.DeviceIdType.MESH
F32 = jnp.float32
BF16 = jnp.bfloat16
SIZES = dict(y=4, zh=4, c=2, zl=4, x=4)


def offsets(*axes):
    steps = itertools.product(*[range(SIZES[a]) for a in axes])
    return [dict(zip(axes, s)) for s in steps if any(s)]


YC = offsets("y", "c")
ZH = offsets("zh")
ZL = offsets("zl")
X = offsets("x")
XY = offsets("x", "y")
XS = [dict(x=d) for d in (1, 3, 2)]
YS = [dict(y=d) for d in (1, 3, 2)]
PEERS = YC + ZH + ZL + [o for o in XY if o["x"]]


def cosine(index):
    t = (jnp.abs(index - 1024) - 512).astype(F32) * (math.pi / 1024)
    s = t * t
    poly = -1.0 / 39916800
    for term in (1.0 / 362880, -1.0 / 5040, 1.0 / 120, -1.0 / 6, 1.0):
        poly = poly * s + term
    return t * poly


def kernel(
    lines, scale, load_hbm, nf_hbm, dm_hbm, modes_hbm, ev_hbm, re_hbm, bc_hbm, out_ref, gd_ref,
    load, nf, dm, stress, ev, re, bc, spec, zspec, usnd, vsnd, urcv, vrcv, own, cbuf, ksnd, kx, kz, kbuf, pu, pv,
    lbuf, dl, gbuf, dbuf, dcore, tab, hr_ref, hi_ref, qr_ref, qi_ref, fwd_ref,
    in_sem, os, orr, c1s, c1r, c2s, c2r, p1s, p1r, v1s, v1r, kxs, kxr, kzs, kzr, kas, kar, kcs, kcr,
    p2s, p2r, v2s, v2r, ls, lr, dls, dlr, gs, gr, ds, dr, gcs, gcr, dcs, dcr,
):
    fpos = lax.axis_index("freq")
    rpos = lax.axis_index("row")
    me = dict(y=fpos // 8, zh=lax.rem(fpos // 2, 4), c=lax.rem(fpos, 2), zl=rpos // 4, x=lax.rem(rpos, 4))
    y, zh, c, zl, x = me["y"], me["zh"], me["c"], me["zl"], me["x"]
    yc = 2 * y + c
    sent = []

    def at(off):
        return {k: lax.rem(me[k] + off[k], SIZES[k]) if off.get(k) else me[k] for k in SIZES}

    def ident(o):
        return {"freq": o["y"] * 8 + o["zh"] * 2 + o["c"], "row": o["zl"] * 4 + o["x"]}

    def copy_to(src, dst, ssem, rsem, device):
        return pltpu.make_async_remote_copy(
            src_ref=src, dst_ref=dst, send_sem=ssem, recv_sem=rsem, device_id=device, device_id_type=MESH
        )

    def send(src, dst, ssem, rsem, off):
        copy = copy_to(src, dst, ssem, rsem, ident(at(off)))
        copy.start()
        sent.append(copy)
        return copy

    def arrive(copies):
        for copy in copies:
            copy.wait_recv()

    owner = {"freq": zl * 8 + x * 2 + y // 2, "row": rpos}
    orphan = fpos != owner["freq"]
    serves = jnp.logical_and(y == zl, zh == x)
    wards = jnp.where(serves, jnp.where(y // 2 == c, 15, 16), 0)

    barrier = pltpu.get_barrier_semaphore()
    for off in ZH + ZL + YC + [o for o in XY if o["x"]]:
        pl.semaphore_signal(barrier, inc=1, device_id=ident(at(off)), device_id_type=MESH)

    @pl.when(orphan)
    def _():
        pl.semaphore_signal(barrier, inc=1, device_id=owner, device_id_type=MESH)

    modes = nf.shape[0]
    local = [
        pltpu.make_async_copy(src, dst, in_sem.at[i])
        for i, (src, dst) in enumerate([
            (nf_hbm, nf), (dm_hbm, dm), (bc_hbm, bc), (load_hbm, load),
            (re_hbm, re), (ev_hbm, ev), (modes_hbm, stress.at[pl.ds(0, modes)]),
        ])
    ]
    for cp in local:
        cp.start()

    row = lax.broadcasted_iota(jnp.int32, (64, 512), 0)
    lane = lax.broadcasted_iota(jnp.int32, (64, 512), 1)
    ph = jnp.bitwise_and((64 * fpos + (lane % 256) // 4) * (64 * rpos + row) + 512 * (lane // 256), 2047)
    fwd = cosine(ph).reshape(8, 1, 8, 512)
    fwd = jnp.broadcast_to(fwd, (8, 4, 8, 512)).reshape(256, 512)
    row = lax.broadcasted_iota(jnp.int32, (256, 512), 0)
    lane = lax.broadcasted_iota(jnp.int32, (256, 512), 1)
    fwd = jnp.where((row // 8) % 4 == lane % 4, fwd, 0.0).astype(BF16)

    for cp in local[:4]:
        cp.wait()
    row = lax.broadcasted_iota(jnp.int32, (256, modes), 0)
    wf = (2 * (64 * fpos + row // 4) + 1).astype(F32) * (1.0 / lines)
    wm = nf[...].reshape(1, modes)
    wm2 = wm * wm
    den_real = wm2 - wf * wf
    den_imag = 2.0 * dm[...].reshape(1, modes) * wm * wf
    gain = wm2 / (den_real * den_real + den_imag * den_imag)
    h_real = gain * den_real
    h_imag = -gain * den_imag
    hr_ref[...] = h_real
    hi_ref[...] = h_imag
    l_real = load[0].astype(F32).reshape(256, modes)
    l_imag = load[1].astype(F32).reshape(256, modes)
    q_real = l_real * h_real - l_imag * h_imag
    q_imag = l_real * h_imag + l_imag * h_real
    spec[pl.ds(0, 256), :] = q_real.astype(BF16)
    spec[pl.ds(256, 256), :] = q_imag.astype(BF16)
    qr_ref[...] = q_real
    qi_ref[...] = q_imag
    usnd[...] = jnp.dot(fwd, spec[...], preferred_element_type=F32).astype(BF16).reshape(8, 32, modes)
    fwd_ref[...] = fwd
    urcv[yc] = usnd[yc]
    for b in range(2):
        cbuf[zh, yc, pl.ds(b, 1), :] = jnp.full((1, 128), bc[b], jnp.int32).astype(F32)


    pl.semaphore_wait(barrier, len(PEERS) + wards)

    served = []
    for i, (dz, dy, e) in enumerate(itertools.product((2, 1, 3, 0), range(2), range(2))):
        target = (2 * c + dy) * 8 + lax.rem(zh + dz, 4) * 2 + e
        served.append((target, copy_to(cbuf.at[zh, yc], own, os.at[i], orr, {"freq": target, "row": rpos})))

    @pl.when(serves)
    def _():
        for target, cp in served:
            @pl.when(target != fpos)
            def _(cp=cp):
                cp.start()

    p1 = []
    for i, o in enumerate(YC):
        t = at(o)
        p1.append(send(usnd.at[2 * t["y"] + t["c"]], urcv.at[yc], p1s.at[i], p1r.at[i], o))

    for cp in local[4:]:
        cp.wait()
    elem = re[...].reshape(1, re.shape[0]) - rpos * ev.shape[0]
    eye = lax.broadcasted_iota(jnp.int32, (128, 128), 0) == lax.broadcasted_iota(jnp.int32, (128, 128), 1)
    vol = jnp.broadcast_to(ev[...].reshape(1, 128), (128, 128))
    vol = jnp.sum(jnp.where(eye, vol, 0.0), axis=1, keepdims=True)
    onehot = lax.broadcasted_iota(jnp.int32, (128, elem.shape[1]), 0) == elem
    weight = jnp.sum(jnp.where(onehot, vol, 0.0), axis=0, keepdims=True) * (2.0 * scale)
    stress[pl.ds(modes, 768 - modes), :] = jnp.zeros((768 - modes, stress.shape[1]), BF16)
    part = stress[pl.ds(pl.multiple_of(96 * yc, 32), 96), :].astype(F32) * weight
    kpart = lax.dot_general(
        part.astype(BF16), stress[pl.ds(0, modes), :], (((1,), (1,)), ((), ())), preferred_element_type=F32
    )
    ksnd[...] = kpart.reshape(4, 3, 8, modes).astype(BF16)
    kx[x] = ksnd[x]
    kxc = [send(ksnd.at[at(o)["x"]], kx.at[x], kxs.at[i], kxr.at[i], o) for i, o in enumerate(X)]

    row = lax.broadcasted_iota(jnp.int32, (256, modes), 0)
    ratio = (2 * (64 * fpos + row // 4) + 1).astype(F32) * (2.0 / lines) / nf[...].reshape(1, modes)
    zspec[pl.ds(0, 256), :] = (ratio * (qr_ref[...] * hi_ref[...] + qi_ref[...] * hr_ref[...])).astype(BF16)
    zspec[pl.ds(256, 256), :] = (ratio * (qi_ref[...] * hi_ref[...] - qr_ref[...] * hr_ref[...])).astype(BF16)
    vsnd[...] = jnp.dot(fwd_ref[...], zspec[...], preferred_element_type=F32).astype(BF16).reshape(8, 32, modes)
    vrcv[yc] = vsnd[yc]
    v1 = []
    for i, o in enumerate(YC):
        t = at(o)
        v1.append(send(vsnd.at[2 * t["y"] + t["c"]], vrcv.at[yc], v1s.at[i], v1r.at[i], o))
    c1 = [send(cbuf.at[zh, yc], cbuf.at[zh, yc], c1s.at[i], c1r.at[i], o) for i, o in enumerate(YC)]

    arrive(kxc)
    kz[zl] = jnp.sum(kx[...].astype(F32), axis=0).astype(BF16)
    kzc = [send(kz.at[zl], kz.at[zl], kzs.at[i], kzr.at[i], o) for i, o in enumerate(ZL)]

    arrive(p1)
    usum = jnp.sum(urcv[...].astype(F32), axis=0)

    @pl.when(orphan)
    def _():
        copy_to(cbuf.at[zh, yc], own, os.at[0], orr, owner).wait_recv()

    @pl.when(jnp.logical_not(orphan))
    def _():
        own[...] = cbuf[zh, yc]

    case = jnp.where(lax.rem(y, 2) == 0, own[0:1, 0:1], own[1:2, 0:1])

    def pick(rows):
        sel = jnp.zeros((8, modes), F32)
        for k in range(4):
            sel = jnp.where(case == k, rows[8 * k:8 * k + 8], sel)
        return sel.astype(BF16)

    pu[zh] = pick(usum)
    p2 = [send(pu.at[zh], pu.at[zh], p2s.at[i], p2r.at[i], o) for i, o in enumerate(ZH)]
    arrive(kzc)
    kbuf[y, c, x] = jnp.sum(kz[...].astype(F32), axis=0).astype(BF16)
    kac = [send(kbuf.at[y, c, x], kbuf.at[y, c, x], kas.at[i], kar.at[i], o) for i, o in enumerate(XY)]
    arrive(p2)
    factor = float(lines) ** -0.5
    usel = (jnp.sum(pu[...].astype(F32), axis=0) * factor).astype(BF16)
    lbuf[zl] = usel
    lc = [send(lbuf.at[zl], lbuf.at[zl], ls.at[i], lr.at[i], o) for i, o in enumerate(ZL)]
    arrive(v1)
    pv[zh] = pick(jnp.sum(vrcv[...].astype(F32), axis=0))
    v2 = [send(pv.at[zh], pv.at[zh], v2s.at[i], v2r.at[i], o) for i, o in enumerate(ZH)]
    arrive(c1)
    c2 = [send(cbuf.at[zh], cbuf.at[zh], c2s.at[i], c2r.at[i], o) for i, o in enumerate(ZH)]
    arrive(lc)

    slot = 4 * x + y

    def origin(o):
        return 4 * lax.rem(x + 4 - o.get("x", 0), 4) + lax.rem(y + 4 - o.get("y", 0), 4)

    def sibling(b, i):
        return send(gbuf.at[c, b], gbuf.at[c, b], gcs.at[i], gcr.at[i], dict(c=1))

    gbuf[c, slot] = lbuf[...].astype(F32).reshape(32, modes).astype(BF16)
    first = []
    for i, o in enumerate([XS[0], YS[0], XS[1], YS[1], XS[2], YS[2]]):
        first.append((o, send(gbuf.at[c, slot], gbuf.at[c, slot], gs.at[i], gr.at[i], o)))
    fc = [sibling(slot, 0)]
    arrive(kac)
    kcc = send(kbuf.at[:, c], kbuf.at[:, c], kcs, kcr, dict(c=1))
    second = []
    for o, cp in first:
        arrive([cp])
        b = origin(o)
        half = pl.ds(0 if "x" in o else 16, 16)
        for o2 in YS if "x" in o else XS:
            n = 6 + len(second)
            copy = send(gbuf.at[c, b, half], gbuf.at[c, b, half], gs.at[n], gr.at[n], o2)
            second.append(({**o, **o2}, copy))
        fc.append(sibling(b, len(fc)))

    arrive([kcc])
    kmat = kbuf[...].reshape(32, 24, modes)[0:25].reshape(600, modes)
    g = jnp.dot(usel, kmat, preferred_element_type=F32).astype(BF16).astype(F32)
    arrive(v2)
    dl[zl] = jnp.sum(g * (jnp.sum(pv[...].astype(F32), axis=0) * factor), axis=0, keepdims=True)
    dlc = [send(dl.at[zl], dl.at[zl], dls.at[i], dlr.at[i], o) for i, o in enumerate(ZL)]

    arrive(c2)
    spread = (
        lax.broadcasted_iota(jnp.int32, (512, 128), 0) // 4 == lax.broadcasted_iota(jnp.int32, (512, 128), 1)
    ).astype(BF16)
    rcase = (lax.broadcasted_iota(jnp.int32, (512, 128), 0) % 4).astype(F32)
    trow = lax.broadcasted_iota(jnp.int32, (128, 128), 0)
    tlane = lax.broadcasted_iota(jnp.int32, (128, 128), 1)
    clane = lax.broadcasted_iota(jnp.int32, (1, 128), 1)
    for xs in range(4):
        cases = jnp.zeros((1, 128), F32)
        for ys in range(4):
            for zs in range(4):
                mine = jnp.logical_and(clane // 32 == ys, (clane // 8) % 4 == zs)
                cases = jnp.where(mine, cbuf[xs, 2 * zs + ys // 2, pl.ds(ys % 2, 1), :], cases)
        keep = rcase == cases
        for cs in range(2):
            n = 64 * (4 * ((tlane // 8) % 4) + xs) + 8 * (2 * (tlane // 32) + cs) + tlane % 8
            ph = jnp.bitwise_and((64 * fpos + trow % 64) * n + 512 * (trow // 64), 2047)
            wide = jnp.dot(spread, cosine(ph).astype(BF16), preferred_element_type=F32)
            tab[cs, :, pl.ds(128 * xs, 128)] = jnp.where(keep, wide, 0.0).astype(BF16)

    arrive(dlc)
    dbuf[slot] = jnp.sum(dl[...], axis=0)
    dc = [send(dbuf.at[slot], dbuf.at[slot], ds.at[i], dr.at[i], o) for i, o in enumerate(XY)]
    halves = {}
    for o, cp in second:
        arrive([cp])
        key = (o["x"], o["y"])
        halves[key] = halves.get(key, 0) + 1
        if halves[key] == 2:
            fc.append(sibling(origin(o), len(fc)))
    gt = jnp.dot(tab[c], gbuf[c].reshape(512, modes), preferred_element_type=F32)
    arrive(dc)
    dcore[c] = jnp.sum(dbuf[...], axis=0)
    dcc = send(dcore.at[c], dcore.at[c], dcs, dcr, dict(c=1))
    arrive(fc)
    gt += jnp.dot(tab[1 - c], gbuf[1 - c].reshape(512, modes), preferred_element_type=F32)
    gq = jnp.dot(gt.astype(BF16), kmat, preferred_element_type=F32) * factor
    h_real = hr_ref[...]
    h_imag = hi_ref[...]
    out_ref[0] = (gq[0:256] * h_real + gq[256:512] * h_imag).reshape(64, 4, modes)
    out_ref[1] = (gq[256:512] * h_real - gq[0:256] * h_imag).reshape(64, 4, modes)
    arrive([dcc])
    gd_ref[...] = (dcore[0] + dcore[1]).reshape(modes)

    @pl.when(serves)
    def _():
        for target, cp in served:
            @pl.when(target != fpos)
            def _(cp=cp):
                cp.wait_send()

    for cp in sent:
        cp.wait_send()


def per_device(spectral_load, natural_freq, damping, stress_modes, element_volume, row_element, block_case):
    _, freq_dev, cases, modes = spectral_load.shape
    lines = freq_dev * lax.axis_size("freq")
    rows = stress_modes.shape[1]
    times = block_case.shape[0] * TBL * lax.axis_size("freq")
    scale = float(modes * lines) / float(rows * lax.axis_size("row") * times)
    hbm = pl.BlockSpec(memory_space=pltpu.HBM)
    vmem = pl.BlockSpec(memory_space=pltpu.VMEM)
    dma = pltpu.SemaphoreType.DMA
    pairs = [7, 3, 7, 7, 3, 3, 15, None, 3, 3, 3, 3, 24, 15, 16, None]
    return pl.pallas_call(
        functools.partial(kernel, lines, scale),
        out_shape=(
            jax.ShapeDtypeStruct((2, freq_dev, cases, modes), F32),
            jax.ShapeDtypeStruct((modes,), F32),
        ),
        in_specs=[hbm] * 7,
        out_specs=(vmem, vmem),
        scratch_shapes=[
            pltpu.VMEM((2, freq_dev, cases, modes), BF16),
            pltpu.VMEM((modes,), F32),
            pltpu.VMEM((modes,), F32),
            pltpu.VMEM((768, rows), BF16),
            pltpu.VMEM(element_volume.shape, F32),
            pltpu.VMEM(row_element.shape, jnp.int32),
            pltpu.SMEM(block_case.shape, jnp.int32),
            pltpu.VMEM((512, modes), BF16),
            pltpu.VMEM((512, modes), BF16),
            pltpu.VMEM((8, 32, modes), BF16),
            pltpu.VMEM((8, 32, modes), BF16),
            pltpu.VMEM((8, 32, modes), BF16),
            pltpu.VMEM((8, 32, modes), BF16),
            pltpu.VMEM((2, 128), F32),
            pltpu.VMEM((4, 8, 2, 128), F32),
            pltpu.VMEM((4, 3, 8, modes), BF16),
            pltpu.VMEM((4, 3, 8, modes), BF16),
            pltpu.VMEM((4, 3, 8, modes), BF16),
            pltpu.VMEM((4, 2, 4, 3, 8, modes), BF16),
            pltpu.VMEM((4, 8, modes), BF16),
            pltpu.VMEM((4, 8, modes), BF16),
            pltpu.VMEM((4, 8, modes), BF16),
            pltpu.VMEM((4, 1, modes), F32),
            pltpu.VMEM((2, 16, 32, modes), BF16),
            pltpu.VMEM((16, 1, modes), F32),
            pltpu.VMEM((2, 1, modes), F32),
            pltpu.VMEM((2, 512, 512), BF16),
            pltpu.VMEM((256, modes), F32),
            pltpu.VMEM((256, modes), F32),
            pltpu.VMEM((256, modes), F32),
            pltpu.VMEM((256, modes), F32),
            pltpu.VMEM((256, 512), BF16),
            dma((7,)), dma((16,)), dma,
        ] + [dma if s is None else dma((s,)) for s in pairs for _ in range(2)],
        compiler_params=pltpu.CompilerParams(
            collective_id=0, has_side_effects=True, vmem_limit_bytes=40 * 1024 * 1024
        ),
        name="adjoint",
    )(*[
        pltpu.with_memory_space_constraint(a, pltpu.HBM)
        for a in (spectral_load, natural_freq, damping, stress_modes, element_volume, row_element, block_case)
    ])


def solution(mesh):
    return jax.shard_map(
        per_device,
        mesh=mesh,
        in_specs=(
            P(None, "freq", None, None),
            P(),
            P(),
            P(None, "row"),
            P("row"),
            P("row"),
            P("freq"),
        ),
        out_specs=(P(None, "freq", None, None), P()),
        check_vma=False,
    )
```

```python
import functools
import itertools
import math

import jax
import jax.numpy as jnp
from jax import lax
from jax.experimental import pallas as pl
from jax.experimental.pallas import tpu as pltpu
from jax.sharding import PartitionSpec as P

TBL = 16
MESH = pl.DeviceIdType.MESH
F32 = jnp.float32
BF16 = jnp.bfloat16
SIZES = dict(y=4, zh=4, c=2, zl=4, x=4)


def offsets(*axes):
    steps = itertools.product(*[range(SIZES[a]) for a in axes])
    return [dict(zip(axes, s)) for s in steps if any(s)]


YC = offsets("y", "c")
ZH = offsets("zh")
ZL = offsets("zl")
X = offsets("x")
XY = offsets("x", "y")
XS = [dict(x=d) for d in (1, 3, 2)]
YS = [dict(y=d) for d in (1, 3, 2)]
Z = offsets("zh", "zl")
PEERS = ZH + [o for o in Z if o["zl"]] + YC + [o for o in XY if o["x"]]


def cosine(index):
    t = (jnp.abs(index - 1024) - 512).astype(F32) * (math.pi / 1024)
    s = t * t
    poly = -1.0 / 39916800
    for term in (1.0 / 362880, -1.0 / 5040, 1.0 / 120, -1.0 / 6, 1.0):
        poly = poly * s + term
    return t * poly


def kernel(
    lines, scale, load_hbm, nf_hbm, dm_hbm, modes_hbm, ev_hbm, re_hbm, bc_hbm, out_ref, gd_ref,
    load, nf, dm, stress, ev, re, bc, spec, zspec, usnd, vsnd, urcv, vrcv, own, cbuf, ksnd, kx, kz, kbuf, pu,
    lbuf, dl, gbuf, dbuf, dcore, tab, hr_ref, hi_ref, qr_ref, qi_ref, fwd_ref,
    in_sem, os, orr, c1s, c1r, c2s, c2r, p1s, p1r, v1s, v1r, kxs, kxr, kzs, kzr, kas, kar, kcs, kcr,
    p2s, p2r, ls, lr, dls, dlr, gs, gr, ds, dr, gcs, gcr, dcs, dcr,
):
    fpos = lax.axis_index("freq")
    rpos = lax.axis_index("row")
    me = dict(y=fpos // 8, zh=lax.rem(fpos // 2, 4), c=lax.rem(fpos, 2), zl=rpos // 4, x=lax.rem(rpos, 4))
    y, zh, c, zl, x = me["y"], me["zh"], me["c"], me["zl"], me["x"]
    yc = 2 * y + c
    sent = []

    def at(off):
        return {k: lax.rem(me[k] + off[k], SIZES[k]) if off.get(k) else me[k] for k in SIZES}

    def ident(o):
        return {"freq": o["y"] * 8 + o["zh"] * 2 + o["c"], "row": o["zl"] * 4 + o["x"]}

    def copy_to(src, dst, ssem, rsem, device):
        return pltpu.make_async_remote_copy(
            src_ref=src, dst_ref=dst, send_sem=ssem, recv_sem=rsem, device_id=device, device_id_type=MESH
        )

    def send(src, dst, ssem, rsem, off):
        copy = copy_to(src, dst, ssem, rsem, ident(at(off)))
        copy.start()
        sent.append(copy)
        return copy

    def arrive(copies):
        for copy in copies:
            copy.wait_recv()

    owner = {"freq": zl * 8 + x * 2 + y // 2, "row": rpos}
    orphan = fpos != owner["freq"]
    serves = jnp.logical_and(y == zl, zh == x)
    wards = jnp.where(serves, jnp.where(y // 2 == c, 15, 16), 0)

    barrier = pltpu.get_barrier_semaphore()
    for off in PEERS:
        pl.semaphore_signal(barrier, inc=1, device_id=ident(at(off)), device_id_type=MESH)

    @pl.when(orphan)
    def _():
        pl.semaphore_signal(barrier, inc=1, device_id=owner, device_id_type=MESH)

    modes = nf.shape[0]
    local = [
        pltpu.make_async_copy(src, dst, in_sem.at[i])
        for i, (src, dst) in enumerate([
            (nf_hbm, nf), (dm_hbm, dm), (bc_hbm, bc), (load_hbm, load),
            (re_hbm, re), (ev_hbm, ev), (modes_hbm, stress.at[pl.ds(0, modes)]),
        ])
    ]
    for cp in local:
        cp.start()

    row = lax.broadcasted_iota(jnp.int32, (64, 512), 0)
    lane = lax.broadcasted_iota(jnp.int32, (64, 512), 1)
    ph = jnp.bitwise_and((64 * fpos + (lane % 256) // 4) * (64 * rpos + row) + 512 * (lane // 256), 2047)
    fwd = cosine(ph).reshape(8, 1, 8, 512)
    fwd = jnp.broadcast_to(fwd, (8, 4, 8, 512)).reshape(256, 512)
    row = lax.broadcasted_iota(jnp.int32, (256, 512), 0)
    lane = lax.broadcasted_iota(jnp.int32, (256, 512), 1)
    fwd = jnp.where((row // 8) % 4 == lane % 4, fwd, 0.0).astype(BF16)

    for cp in local[:4]:
        cp.wait()
    row = lax.broadcasted_iota(jnp.int32, (256, modes), 0)
    wf = (2 * (64 * fpos + row // 4) + 1).astype(F32) * (1.0 / lines)
    wm = nf[...].reshape(1, modes)
    wm2 = wm * wm
    den_real = wm2 - wf * wf
    den_imag = 2.0 * dm[...].reshape(1, modes) * wm * wf
    gain = wm2 / (den_real * den_real + den_imag * den_imag)
    h_real = gain * den_real
    h_imag = -gain * den_imag
    hr_ref[...] = h_real
    hi_ref[...] = h_imag
    l_real = load[0].astype(F32).reshape(256, modes)
    l_imag = load[1].astype(F32).reshape(256, modes)
    q_real = l_real * h_real - l_imag * h_imag
    q_imag = l_real * h_imag + l_imag * h_real
    spec[pl.ds(0, 256), :] = q_real.astype(BF16)
    spec[pl.ds(256, 256), :] = q_imag.astype(BF16)
    qr_ref[...] = q_real
    qi_ref[...] = q_imag
    usnd[...] = jnp.dot(fwd, spec[...], preferred_element_type=F32).astype(BF16).reshape(8, 32, modes)
    fwd_ref[...] = fwd
    urcv[yc] = usnd[yc]
    for b in range(2):
        cbuf[zh, yc, pl.ds(b, 1), :] = jnp.full((1, 128), bc[b], jnp.int32).astype(F32)


    pl.semaphore_wait(barrier, len(PEERS) + wards)

    served = []
    for i, (dz, dy, e) in enumerate(itertools.product((2, 1, 3, 0), range(2), range(2))):
        target = (2 * c + dy) * 8 + lax.rem(zh + dz, 4) * 2 + e
        served.append((target, copy_to(cbuf.at[zh, yc], own, os.at[i], orr, {"freq": target, "row": rpos})))

    @pl.when(serves)
    def _():
        for target, cp in served:
            @pl.when(target != fpos)
            def _(cp=cp):
                cp.start()

    p1 = []
    for i, o in enumerate(YC):
        t = at(o)
        p1.append(send(usnd.at[2 * t["y"] + t["c"]], urcv.at[yc], p1s.at[i], p1r.at[i], o))

    for cp in local[4:]:
        cp.wait()
    elem = re[...].reshape(1, re.shape[0]) - rpos * ev.shape[0]
    eye = lax.broadcasted_iota(jnp.int32, (128, 128), 0) == lax.broadcasted_iota(jnp.int32, (128, 128), 1)
    vol = jnp.broadcast_to(ev[...].reshape(1, 128), (128, 128))
    vol = jnp.sum(jnp.where(eye, vol, 0.0), axis=1, keepdims=True)
    onehot = lax.broadcasted_iota(jnp.int32, (128, elem.shape[1]), 0) == elem
    weight = jnp.sum(jnp.where(onehot, vol, 0.0), axis=0, keepdims=True) * (2.0 * scale)
    stress[pl.ds(modes, 768 - modes), :] = jnp.zeros((768 - modes, stress.shape[1]), BF16)
    part = stress[pl.ds(pl.multiple_of(96 * yc, 32), 96), :].astype(F32) * weight
    kpart = lax.dot_general(
        part.astype(BF16), stress[pl.ds(0, modes), :], (((1,), (1,)), ((), ())), preferred_element_type=F32
    )
    ksnd[...] = kpart.reshape(4, 3, 8, modes).astype(BF16)
    kx[x] = ksnd[x]
    kxc = [send(ksnd.at[at(o)["x"]], kx.at[x], kxs.at[i], kxr.at[i], o) for i, o in enumerate(X)]

    row = lax.broadcasted_iota(jnp.int32, (256, modes), 0)
    ratio = (2 * (64 * fpos + row // 4) + 1).astype(F32) * (2.0 / lines) / nf[...].reshape(1, modes)
    zspec[pl.ds(0, 256), :] = (ratio * (qr_ref[...] * hi_ref[...] + qi_ref[...] * hr_ref[...])).astype(BF16)
    zspec[pl.ds(256, 256), :] = (ratio * (qi_ref[...] * hi_ref[...] - qr_ref[...] * hr_ref[...])).astype(BF16)
    vsnd[...] = jnp.dot(fwd_ref[...], zspec[...], preferred_element_type=F32).astype(BF16).reshape(8, 32, modes)
    vrcv[yc] = vsnd[yc]
    v1 = []
    for i, o in enumerate(YC):
        t = at(o)
        v1.append(send(vsnd.at[2 * t["y"] + t["c"]], vrcv.at[yc], v1s.at[i], v1r.at[i], o))
    c1 = [send(cbuf.at[zh, yc], cbuf.at[zh, yc], c1s.at[i], c1r.at[i], o) for i, o in enumerate(YC)]

    arrive(kxc)
    kz[zl] = jnp.sum(kx[...].astype(F32), axis=0).astype(BF16)
    kzc = [send(kz.at[zl], kz.at[zl], kzs.at[i], kzr.at[i], o) for i, o in enumerate(ZL)]

    arrive(p1)
    usum = jnp.sum(urcv[...].astype(F32), axis=0)

    @pl.when(orphan)
    def _():
        copy_to(cbuf.at[zh, yc], own, os.at[0], orr, owner).wait_recv()

    @pl.when(jnp.logical_not(orphan))
    def _():
        own[...] = cbuf[zh, yc]

    case = jnp.where(lax.rem(y, 2) == 0, own[0:1, 0:1], own[1:2, 0:1])

    def pick(rows):
        sel = jnp.zeros((8, modes), F32)
        for k in range(4):
            sel = jnp.where(case == k, rows[8 * k:8 * k + 8], sel)
        return sel

    pu[zh] = pick(usum).astype(BF16)
    p2 = [send(pu.at[zh], pu.at[zh], p2s.at[i], p2r.at[i], o) for i, o in enumerate(ZH)]
    arrive(kzc)
    kbuf[y, c, x] = jnp.sum(kz[...].astype(F32), axis=0).astype(BF16)
    kac = [send(kbuf.at[y, c, x], kbuf.at[y, c, x], kas.at[i], kar.at[i], o) for i, o in enumerate(XY)]
    arrive(p2)
    factor = float(lines) ** -0.5
    usel = (jnp.sum(pu[...].astype(F32), axis=0) * factor).astype(BF16)
    lbuf[zl] = usel
    lc = [send(lbuf.at[zl], lbuf.at[zl], ls.at[i], lr.at[i], o) for i, o in enumerate(ZL)]
    arrive(c1)
    c2 = [send(cbuf.at[zh], cbuf.at[zh], c2s.at[i], c2r.at[i], o) for i, o in enumerate(ZH)]
    arrive(kac)
    kcc = send(kbuf.at[:, c], kbuf.at[:, c], kcs, kcr, dict(c=1))
    arrive(v1)
    vsel = pick(jnp.sum(vrcv[...].astype(F32), axis=0)) * factor
    arrive(lc)

    slot = 4 * x + y

    def origin(o):
        return 4 * lax.rem(x + 4 - o.get("x", 0), 4) + lax.rem(y + 4 - o.get("y", 0), 4)

    def sibling(b, i):
        return send(gbuf.at[c, b], gbuf.at[c, b], gcs.at[i], gcr.at[i], dict(c=1))

    gbuf[c, slot] = lbuf[...].astype(F32).reshape(32, modes).astype(BF16)
    first = []
    for i, o in enumerate([XS[0], YS[0], XS[1], YS[1], XS[2], YS[2]]):
        first.append((o, send(gbuf.at[c, slot], gbuf.at[c, slot], gs.at[i], gr.at[i], o)))
    fc = [sibling(slot, 0)]
    arrive([kcc])
    kmat = kbuf[...].reshape(32, 24, modes)[0:25].reshape(600, modes)
    g = jnp.dot(usel, kmat, preferred_element_type=F32).astype(BF16).astype(F32)
    dl[zh, zl] = jnp.sum(g * vsel, axis=0, keepdims=True)
    dlc = [send(dl.at[zh, zl], dl.at[zh, zl], dls.at[i], dlr.at[i], o) for i, o in enumerate(Z)]
    second = []
    for o, cp in first:
        arrive([cp])
        b = origin(o)
        half = pl.ds(0 if "x" in o else 16, 16)
        for o2 in YS if "x" in o else XS:
            n = 6 + len(second)
            copy = send(gbuf.at[c, b, half], gbuf.at[c, b, half], gs.at[n], gr.at[n], o2)
            second.append(({**o, **o2}, copy))
        fc.append(sibling(b, len(fc)))

    arrive(c2)
    spread = (
        lax.broadcasted_iota(jnp.int32, (512, 128), 0) // 4 == lax.broadcasted_iota(jnp.int32, (512, 128), 1)
    ).astype(BF16)
    rcase = (lax.broadcasted_iota(jnp.int32, (512, 128), 0) % 4).astype(F32)
    trow = lax.broadcasted_iota(jnp.int32, (128, 128), 0)
    tlane = lax.broadcasted_iota(jnp.int32, (128, 128), 1)
    clane = lax.broadcasted_iota(jnp.int32, (1, 128), 1)
    for xs in range(4):
        cases = jnp.zeros((1, 128), F32)
        for ys in range(4):
            for zs in range(4):
                mine = jnp.logical_and(clane // 32 == ys, (clane // 8) % 4 == zs)
                cases = jnp.where(mine, cbuf[xs, 2 * zs + ys // 2, pl.ds(ys % 2, 1), :], cases)
        keep = rcase == cases
        for cs in range(2):
            n = 64 * (4 * ((tlane // 8) % 4) + xs) + 8 * (2 * (tlane // 32) + cs) + tlane % 8
            ph = jnp.bitwise_and((64 * fpos + trow % 64) * n + 512 * (trow // 64), 2047)
            wide = jnp.dot(spread, cosine(ph).astype(BF16), preferred_element_type=F32)
            tab[cs, :, pl.ds(128 * xs, 128)] = jnp.where(keep, wide, 0.0).astype(BF16)

    arrive(dlc)
    dbuf[slot] = jnp.sum(dl[...], axis=(0, 1))
    dc = [send(dbuf.at[slot], dbuf.at[slot], ds.at[i], dr.at[i], o) for i, o in enumerate(XY)]
    halves = {}
    for o, cp in second:
        arrive([cp])
        key = (o["x"], o["y"])
        halves[key] = halves.get(key, 0) + 1
        if halves[key] == 2:
            fc.append(sibling(origin(o), len(fc)))
    gt = jnp.dot(tab[c], gbuf[c].reshape(512, modes), preferred_element_type=F32)
    arrive(dc)
    dcore[c] = jnp.sum(dbuf[...], axis=0)
    dcc = send(dcore.at[c], dcore.at[c], dcs, dcr, dict(c=1))
    arrive(fc)
    gt += jnp.dot(tab[1 - c], gbuf[1 - c].reshape(512, modes), preferred_element_type=F32)
    gq = jnp.dot(gt.astype(BF16), kmat, preferred_element_type=F32) * factor
    h_real = hr_ref[...]
    h_imag = hi_ref[...]
    out_ref[0] = (gq[0:256] * h_real + gq[256:512] * h_imag).reshape(64, 4, modes)
    out_ref[1] = (gq[256:512] * h_real - gq[0:256] * h_imag).reshape(64, 4, modes)
    arrive([dcc])
    gd_ref[...] = (dcore[0] + dcore[1]).reshape(modes)

    @pl.when(serves)
    def _():
        for target, cp in served:
            @pl.when(target != fpos)
            def _(cp=cp):
                cp.wait_send()

    for cp in sent:
        cp.wait_send()


def per_device(spectral_load, natural_freq, damping, stress_modes, element_volume, row_element, block_case):
    _, freq_dev, cases, modes = spectral_load.shape
    lines = freq_dev * lax.axis_size("freq")
    rows = stress_modes.shape[1]
    times = block_case.shape[0] * TBL * lax.axis_size("freq")
    scale = float(modes * lines) / float(rows * lax.axis_size("row") * times)
    hbm = pl.BlockSpec(memory_space=pltpu.HBM)
    vmem = pl.BlockSpec(memory_space=pltpu.VMEM)
    dma = pltpu.SemaphoreType.DMA
    pairs = [7, 3, 7, 7, 3, 3, 15, None, 3, 3, 15, 24, 15, 16, None]
    return pl.pallas_call(
        functools.partial(kernel, lines, scale),
        out_shape=(
            jax.ShapeDtypeStruct((2, freq_dev, cases, modes), F32),
            jax.ShapeDtypeStruct((modes,), F32),
        ),
        in_specs=[hbm] * 7,
        out_specs=(vmem, vmem),
        scratch_shapes=[
            pltpu.VMEM((2, freq_dev, cases, modes), BF16),
            pltpu.VMEM((modes,), F32),
            pltpu.VMEM((modes,), F32),
            pltpu.VMEM((768, rows), BF16),
            pltpu.VMEM(element_volume.shape, F32),
            pltpu.VMEM(row_element.shape, jnp.int32),
            pltpu.SMEM(block_case.shape, jnp.int32),
            pltpu.VMEM((512, modes), BF16),
            pltpu.VMEM((512, modes), BF16),
            pltpu.VMEM((8, 32, modes), BF16),
            pltpu.VMEM((8, 32, modes), BF16),
            pltpu.VMEM((8, 32, modes), BF16),
            pltpu.VMEM((8, 32, modes), BF16),
            pltpu.VMEM((2, 128), F32),
            pltpu.VMEM((4, 8, 2, 128), F32),
            pltpu.VMEM((4, 3, 8, modes), BF16),
            pltpu.VMEM((4, 3, 8, modes), BF16),
            pltpu.VMEM((4, 3, 8, modes), BF16),
            pltpu.VMEM((4, 2, 4, 3, 8, modes), BF16),
            pltpu.VMEM((4, 8, modes), BF16),
            pltpu.VMEM((4, 8, modes), BF16),
            pltpu.VMEM((4, 4, 1, modes), F32),
            pltpu.VMEM((2, 16, 32, modes), BF16),
            pltpu.VMEM((16, 1, modes), F32),
            pltpu.VMEM((2, 1, modes), F32),
            pltpu.VMEM((2, 512, 512), BF16),
            pltpu.VMEM((256, modes), F32),
            pltpu.VMEM((256, modes), F32),
            pltpu.VMEM((256, modes), F32),
            pltpu.VMEM((256, modes), F32),
            pltpu.VMEM((256, 512), BF16),
            dma((7,)), dma((16,)), dma,
        ] + [dma if s is None else dma((s,)) for s in pairs for _ in range(2)],
        compiler_params=pltpu.CompilerParams(
            collective_id=0, has_side_effects=True, vmem_limit_bytes=40 * 1024 * 1024
        ),
        name="adjoint",
    )(*[
        pltpu.with_memory_space_constraint(a, pltpu.HBM)
        for a in (spectral_load, natural_freq, damping, stress_modes, element_volume, row_element, block_case)
    ])


def solution(mesh):
    return jax.shard_map(
        per_device,
        mesh=mesh,
        in_specs=(
            P(None, "freq", None, None),
            P(),
            P(),
            P(None, "row"),
            P("row"),
            P("row"),
            P("freq"),
        ),
        out_specs=(P(None, "freq", None, None), P()),
        check_vma=False,
    )
```

```python
import functools
import itertools
import math

import jax
import jax.numpy as jnp
from jax import lax
from jax.experimental import pallas as pl
from jax.experimental.pallas import tpu as pltpu
from jax.sharding import PartitionSpec as P

TBL = 16
MESH = pl.DeviceIdType.MESH
F32 = jnp.float32
BF16 = jnp.bfloat16
SIZES = dict(y=4, zh=4, c=2, zl=4, x=4)


def offsets(*axes):
    steps = itertools.product(*[range(SIZES[a]) for a in axes])
    return [dict(zip(axes, s)) for s in steps if any(s)]


YC = offsets("y", "c")
ZH = offsets("zh")
ZL = offsets("zl")
X = offsets("x")
XY = offsets("x", "y")
XS = [dict(x=d) for d in (1, 3, 2)]
YS = [dict(y=d) for d in (1, 3, 2)]
Z = offsets("zh", "zl")
PEERS = ZH + [o for o in Z if o["zl"]] + YC + [o for o in XY if o["x"]]


def cosine(index):
    t = (jnp.abs(index - 1024) - 512).astype(F32) * (math.pi / 1024)
    s = t * t
    poly = -1.0 / 39916800
    for term in (1.0 / 362880, -1.0 / 5040, 1.0 / 120, -1.0 / 6, 1.0):
        poly = poly * s + term
    return t * poly


def kernel(
    lines, scale, load_hbm, nf_hbm, dm_hbm, modes_hbm, ev_hbm, re_hbm, bc_hbm, gq_ref, gd_ref, hr_ref, hi_ref,
    load, nf, dm, stress, ev, re, bc, spec, zspec, usnd, vsnd, urcv, vrcv, own, cbuf, ksnd, kx, kz, kbuf, pu,
    lbuf, dl, gbuf, dbuf, dcore, tab, qr_ref, qi_ref, fwd_ref,
    in_sem, os, orr, c1s, c1r, c2s, c2r, p1s, p1r, v1s, v1r, kxs, kxr, kzs, kzr, kas, kar, kcs, kcr,
    p2s, p2r, ls, lr, dls, dlr, gs, gr, ds, dr, gcs, gcr, dcs, dcr,
):
    fpos = lax.axis_index("freq")
    rpos = lax.axis_index("row")
    me = dict(y=fpos // 8, zh=lax.rem(fpos // 2, 4), c=lax.rem(fpos, 2), zl=rpos // 4, x=lax.rem(rpos, 4))
    y, zh, c, zl, x = me["y"], me["zh"], me["c"], me["zl"], me["x"]
    yc = 2 * y + c
    sent = []

    def at(off):
        return {k: lax.rem(me[k] + off[k], SIZES[k]) if off.get(k) else me[k] for k in SIZES}

    def ident(o):
        return {"freq": o["y"] * 8 + o["zh"] * 2 + o["c"], "row": o["zl"] * 4 + o["x"]}

    def copy_to(src, dst, ssem, rsem, device):
        return pltpu.make_async_remote_copy(
            src_ref=src, dst_ref=dst, send_sem=ssem, recv_sem=rsem, device_id=device, device_id_type=MESH
        )

    def send(src, dst, ssem, rsem, off):
        copy = copy_to(src, dst, ssem, rsem, ident(at(off)))
        copy.start()
        sent.append(copy)
        return copy

    def arrive(copies):
        for copy in copies:
            copy.wait_recv()

    owner = {"freq": zl * 8 + x * 2 + y // 2, "row": rpos}
    orphan = fpos != owner["freq"]
    serves = jnp.logical_and(y == zl, zh == x)
    wards = jnp.where(serves, jnp.where(y // 2 == c, 15, 16), 0)

    barrier = pltpu.get_barrier_semaphore()
    for off in PEERS:
        pl.semaphore_signal(barrier, inc=1, device_id=ident(at(off)), device_id_type=MESH)

    @pl.when(orphan)
    def _():
        pl.semaphore_signal(barrier, inc=1, device_id=owner, device_id_type=MESH)

    modes = nf.shape[0]
    local = [
        pltpu.make_async_copy(src, dst, in_sem.at[i])
        for i, (src, dst) in enumerate([
            (nf_hbm, nf), (dm_hbm, dm), (bc_hbm, bc), (load_hbm, load),
            (re_hbm, re), (ev_hbm, ev), (modes_hbm, stress.at[pl.ds(0, modes)]),
        ])
    ]
    for cp in local:
        cp.start()

    row = lax.broadcasted_iota(jnp.int32, (64, 512), 0)
    lane = lax.broadcasted_iota(jnp.int32, (64, 512), 1)
    ph = jnp.bitwise_and((64 * fpos + (lane % 256) // 4) * (64 * rpos + row) + 512 * (lane // 256), 2047)
    fwd = cosine(ph).reshape(8, 1, 8, 512)
    fwd = jnp.broadcast_to(fwd, (8, 4, 8, 512)).reshape(256, 512)
    row = lax.broadcasted_iota(jnp.int32, (256, 512), 0)
    lane = lax.broadcasted_iota(jnp.int32, (256, 512), 1)
    fwd = jnp.where((row // 8) % 4 == lane % 4, fwd, 0.0).astype(BF16)

    for cp in local[:4]:
        cp.wait()
    row = lax.broadcasted_iota(jnp.int32, (256, modes), 0)
    wf = (2 * (64 * fpos + row // 4) + 1).astype(F32) * (1.0 / lines)
    wm = nf[...].reshape(1, modes)
    wm2 = wm * wm
    den_real = wm2 - wf * wf
    den_imag = 2.0 * dm[...].reshape(1, modes) * wm * wf
    gain = wm2 / (den_real * den_real + den_imag * den_imag)
    h_real = gain * den_real
    h_imag = -gain * den_imag
    hr_ref[...] = h_real
    hi_ref[...] = h_imag
    l_real = load[0].astype(F32).reshape(256, modes)
    l_imag = load[1].astype(F32).reshape(256, modes)
    q_real = l_real * h_real - l_imag * h_imag
    q_imag = l_real * h_imag + l_imag * h_real
    spec[pl.ds(0, 256), :] = q_real.astype(BF16)
    spec[pl.ds(256, 256), :] = q_imag.astype(BF16)
    qr_ref[...] = q_real
    qi_ref[...] = q_imag
    usnd[...] = jnp.dot(fwd, spec[...], preferred_element_type=F32).astype(BF16).reshape(8, 32, modes)
    fwd_ref[...] = fwd
    urcv[yc] = usnd[yc]
    for b in range(2):
        cbuf[zh, yc, pl.ds(b, 1), :] = jnp.full((1, 128), bc[b], jnp.int32).astype(F32)

    for cp in local[4:]:
        cp.wait()
    elem = re[...].reshape(1, re.shape[0]) - rpos * ev.shape[0]
    eye = lax.broadcasted_iota(jnp.int32, (128, 128), 0) == lax.broadcasted_iota(jnp.int32, (128, 128), 1)
    vol = jnp.broadcast_to(ev[...].reshape(1, 128), (128, 128))
    vol = jnp.sum(jnp.where(eye, vol, 0.0), axis=1, keepdims=True)
    onehot = lax.broadcasted_iota(jnp.int32, (128, elem.shape[1]), 0) == elem
    weight = jnp.sum(jnp.where(onehot, vol, 0.0), axis=0, keepdims=True) * (2.0 * scale)
    stress[pl.ds(modes, 768 - modes), :] = jnp.zeros((768 - modes, stress.shape[1]), BF16)
    part = stress[pl.ds(pl.multiple_of(96 * yc, 32), 96), :].astype(F32) * weight
    kpart = lax.dot_general(
        part.astype(BF16), stress[pl.ds(0, modes), :], (((1,), (1,)), ((), ())), preferred_element_type=F32
    )
    ksnd[...] = kpart.reshape(4, 3, 8, modes).astype(BF16)
    kx[x] = ksnd[x]

    pl.semaphore_wait(barrier, len(PEERS) + wards)

    served = []
    for i, (dz, dy, e) in enumerate(itertools.product((2, 1, 3, 0), range(2), range(2))):
        target = (2 * c + dy) * 8 + lax.rem(zh + dz, 4) * 2 + e
        served.append((target, copy_to(cbuf.at[zh, yc], own, os.at[i], orr, {"freq": target, "row": rpos})))

    @pl.when(serves)
    def _():
        for target, cp in served:
            @pl.when(target != fpos)
            def _(cp=cp):
                cp.start()

    p1 = []
    for i, o in enumerate(YC):
        t = at(o)
        p1.append(send(usnd.at[2 * t["y"] + t["c"]], urcv.at[yc], p1s.at[i], p1r.at[i], o))

    kxc = [send(ksnd.at[at(o)["x"]], kx.at[x], kxs.at[i], kxr.at[i], o) for i, o in enumerate(X)]

    row = lax.broadcasted_iota(jnp.int32, (256, modes), 0)
    ratio = (2 * (64 * fpos + row // 4) + 1).astype(F32) * (2.0 / lines) / nf[...].reshape(1, modes)
    zspec[pl.ds(0, 256), :] = (ratio * (qr_ref[...] * hi_ref[...] + qi_ref[...] * hr_ref[...])).astype(BF16)
    zspec[pl.ds(256, 256), :] = (ratio * (qi_ref[...] * hi_ref[...] - qr_ref[...] * hr_ref[...])).astype(BF16)
    vsnd[...] = jnp.dot(fwd_ref[...], zspec[...], preferred_element_type=F32).astype(BF16).reshape(8, 32, modes)
    vrcv[yc] = vsnd[yc]
    v1 = []
    for i, o in enumerate(YC):
        t = at(o)
        v1.append(send(vsnd.at[2 * t["y"] + t["c"]], vrcv.at[yc], v1s.at[i], v1r.at[i], o))
    c1 = [send(cbuf.at[zh, yc], cbuf.at[zh, yc], c1s.at[i], c1r.at[i], o) for i, o in enumerate(YC)]

    arrive(kxc)
    kz[zl] = jnp.sum(kx[...].astype(F32), axis=0).astype(BF16)
    kzc = [send(kz.at[zl], kz.at[zl], kzs.at[i], kzr.at[i], o) for i, o in enumerate(ZL)]

    arrive(p1)
    usum = jnp.sum(urcv[...].astype(F32), axis=0)

    @pl.when(orphan)
    def _():
        copy_to(cbuf.at[zh, yc], own, os.at[0], orr, owner).wait_recv()

    @pl.when(jnp.logical_not(orphan))
    def _():
        own[...] = cbuf[zh, yc]

    case = jnp.where(lax.rem(y, 2) == 0, own[0:1, 0:1], own[1:2, 0:1])

    def pick(rows):
        sel = jnp.zeros((8, modes), F32)
        for k in range(4):
            sel = jnp.where(case == k, rows[8 * k:8 * k + 8], sel)
        return sel

    pu[zh] = pick(usum).astype(BF16)
    p2 = [send(pu.at[zh], pu.at[zh], p2s.at[i], p2r.at[i], o) for i, o in enumerate(ZH)]
    arrive(kzc)
    kbuf[y, c, x] = jnp.sum(kz[...].astype(F32), axis=0).astype(BF16)
    kac = [send(kbuf.at[y, c, x], kbuf.at[y, c, x], kas.at[i], kar.at[i], o) for i, o in enumerate(XY)]
    arrive(p2)
    factor = float(lines) ** -0.5
    usel = (jnp.sum(pu[...].astype(F32), axis=0) * factor).astype(BF16)
    lbuf[zl] = usel
    lc = [send(lbuf.at[zl], lbuf.at[zl], ls.at[i], lr.at[i], o) for i, o in enumerate(ZL)]
    arrive(kac)
    kcc = send(kbuf.at[:, c], kbuf.at[:, c], kcs, kcr, dict(c=1))
    arrive(v1)
    vsel = pick(jnp.sum(vrcv[...].astype(F32), axis=0)) * factor
    arrive([kcc])
    kmat = kbuf[...].reshape(32, 24, modes)[0:25].reshape(600, modes)
    g = jnp.dot(usel, kmat, preferred_element_type=F32).astype(BF16).astype(F32)
    dl[zh, zl] = jnp.sum(g * vsel, axis=0, keepdims=True)
    dlc = [send(dl.at[zh, zl], dl.at[zh, zl], dls.at[i], dlr.at[i], o) for i, o in enumerate(Z)]
    arrive(c1)
    c2 = [send(cbuf.at[zh], cbuf.at[zh], c2s.at[i], c2r.at[i], o) for i, o in enumerate(ZH)]
    arrive(lc)

    slot = 4 * x + y

    def origin(o):
        return 4 * lax.rem(x + 4 - o.get("x", 0), 4) + lax.rem(y + 4 - o.get("y", 0), 4)

    def sibling(b, i):
        return send(gbuf.at[c, b], gbuf.at[c, b], gcs.at[i], gcr.at[i], dict(c=1))

    gbuf[c, slot] = lbuf[...].astype(F32).reshape(32, modes).astype(BF16)
    first = []
    for i, o in enumerate([XS[0], YS[0], XS[1], YS[1], XS[2], YS[2]]):
        first.append((o, send(gbuf.at[c, slot], gbuf.at[c, slot], gs.at[i], gr.at[i], o)))
    fc = [sibling(slot, 0)]
    second = []
    for o, cp in first:
        arrive([cp])
        b = origin(o)
        half = pl.ds(0 if "x" in o else 16, 16)
        for o2 in YS if "x" in o else XS:
            n = 6 + len(second)
            copy = send(gbuf.at[c, b, half], gbuf.at[c, b, half], gs.at[n], gr.at[n], o2)
            second.append(({**o, **o2}, copy))
        fc.append(sibling(b, len(fc)))

    arrive(c2)
    spread = (
        lax.broadcasted_iota(jnp.int32, (512, 128), 0) // 4 == lax.broadcasted_iota(jnp.int32, (512, 128), 1)
    ).astype(BF16)
    rcase = (lax.broadcasted_iota(jnp.int32, (512, 128), 0) % 4).astype(F32)
    trow = lax.broadcasted_iota(jnp.int32, (128, 128), 0)
    tlane = lax.broadcasted_iota(jnp.int32, (128, 128), 1)
    clane = lax.broadcasted_iota(jnp.int32, (1, 128), 1)
    for xs in range(4):
        cases = jnp.zeros((1, 128), F32)
        for ys in range(4):
            for zs in range(4):
                mine = jnp.logical_and(clane // 32 == ys, (clane // 8) % 4 == zs)
                cases = jnp.where(mine, cbuf[xs, 2 * zs + ys // 2, pl.ds(ys % 2, 1), :], cases)
        keep = rcase == cases
        for cs in range(2):
            n = 64 * (4 * ((tlane // 8) % 4) + xs) + 8 * (2 * (tlane // 32) + cs) + tlane % 8
            ph = jnp.bitwise_and((64 * fpos + trow % 64) * n + 512 * (trow // 64), 2047)
            wide = jnp.dot(spread, cosine(ph).astype(BF16), preferred_element_type=F32)
            tab[cs, :, pl.ds(128 * xs, 128)] = jnp.where(keep, wide, 0.0).astype(BF16)

    arrive(dlc)
    dbuf[slot] = jnp.sum(dl[...], axis=(0, 1))
    dc = [send(dbuf.at[slot], dbuf.at[slot], ds.at[i], dr.at[i], o) for i, o in enumerate(XY)]
    halves = {}
    for o, cp in second:
        arrive([cp])
        key = (o["x"], o["y"])
        halves[key] = halves.get(key, 0) + 1
        if halves[key] == 2:
            fc.append(sibling(origin(o), len(fc)))
    gt = jnp.dot(tab[c], gbuf[c].reshape(512, modes), preferred_element_type=F32)
    arrive(dc)
    dcore[c] = jnp.sum(dbuf[...], axis=0)
    dcc = send(dcore.at[c], dcore.at[c], dcs, dcr, dict(c=1))
    arrive(fc)
    gt += jnp.dot(tab[1 - c], gbuf[1 - c].reshape(512, modes), preferred_element_type=F32)
    gq = jnp.dot(gt.astype(BF16), kmat, preferred_element_type=F32) * factor
    gq_ref[0] = gq[0:256]
    gq_ref[1] = gq[256:512]
    arrive([dcc])
    gd_ref[...] = dcore[0] + dcore[1]

    @pl.when(serves)
    def _():
        for target, cp in served:
            @pl.when(target != fpos)
            def _(cp=cp):
                cp.wait_send()

    for cp in sent:
        cp.wait_send()


def finish(gq, gd, hr, hi, out_hbm, gd_hbm, out, gdv, sems):
    modes = hr.shape[1]
    gdv[...] = gd[...].reshape(modes)
    copies = [pltpu.make_async_copy(gdv, gd_hbm, sems.at[8])]
    copies[0].start()
    for b in range(4):
        rows = pl.ds(64 * b, 64)
        lines = pl.ds(16 * b, 16)
        out[0, lines] = (gq[0, rows, :] * hr[rows, :] + gq[1, rows, :] * hi[rows, :]).reshape(16, 4, modes)
        out[1, lines] = (gq[1, rows, :] * hr[rows, :] - gq[0, rows, :] * hi[rows, :]).reshape(16, 4, modes)
        for k in range(2):
            copy = pltpu.make_async_copy(out.at[k, lines], out_hbm.at[k, lines], sems.at[2 * b + k])
            copy.start()
            copies.append(copy)
    for copy in copies:
        copy.wait()


def per_device(spectral_load, natural_freq, damping, stress_modes, element_volume, row_element, block_case):
    _, freq_dev, cases, modes = spectral_load.shape
    lines = freq_dev * lax.axis_size("freq")
    rows = stress_modes.shape[1]
    times = block_case.shape[0] * TBL * lax.axis_size("freq")
    scale = float(modes * lines) / float(rows * lax.axis_size("row") * times)
    hbm = pl.BlockSpec(memory_space=pltpu.HBM)
    vmem = pl.BlockSpec(memory_space=pltpu.VMEM)
    dma = pltpu.SemaphoreType.DMA
    pairs = [7, 3, 7, 7, 3, 3, 15, None, 3, 3, 15, 24, 15, 16, None]
    gq, gd, hr, hi = pl.pallas_call(
        functools.partial(kernel, lines, scale),
        out_shape=(
            pltpu.VMEM((2, freq_dev * cases, modes), F32),
            pltpu.VMEM((1, modes), F32),
            pltpu.VMEM((freq_dev * cases, modes), F32),
            pltpu.VMEM((freq_dev * cases, modes), F32),
        ),
        in_specs=[hbm] * 7,
        out_specs=(vmem,) * 4,
        scratch_shapes=[
            pltpu.VMEM((2, freq_dev, cases, modes), BF16),
            pltpu.VMEM((modes,), F32),
            pltpu.VMEM((modes,), F32),
            pltpu.VMEM((768, rows), BF16),
            pltpu.VMEM(element_volume.shape, F32),
            pltpu.VMEM(row_element.shape, jnp.int32),
            pltpu.SMEM(block_case.shape, jnp.int32),
            pltpu.VMEM((512, modes), BF16),
            pltpu.VMEM((512, modes), BF16),
            pltpu.VMEM((8, 32, modes), BF16),
            pltpu.VMEM((8, 32, modes), BF16),
            pltpu.VMEM((8, 32, modes), BF16),
            pltpu.VMEM((8, 32, modes), BF16),
            pltpu.VMEM((2, 128), F32),
            pltpu.VMEM((4, 8, 2, 128), F32),
            pltpu.VMEM((4, 3, 8, modes), BF16),
            pltpu.VMEM((4, 3, 8, modes), BF16),
            pltpu.VMEM((4, 3, 8, modes), BF16),
            pltpu.VMEM((4, 2, 4, 3, 8, modes), BF16),
            pltpu.VMEM((4, 8, modes), BF16),
            pltpu.VMEM((4, 8, modes), BF16),
            pltpu.VMEM((4, 4, 1, modes), F32),
            pltpu.VMEM((2, 16, 32, modes), BF16),
            pltpu.VMEM((16, 1, modes), F32),
            pltpu.VMEM((2, 1, modes), F32),
            pltpu.VMEM((2, 512, 512), BF16),
            pltpu.VMEM((256, modes), F32),
            pltpu.VMEM((256, modes), F32),
            pltpu.VMEM((256, 512), BF16),
            dma((7,)), dma((16,)), dma,
        ] + [dma if s is None else dma((s,)) for s in pairs for _ in range(2)],
        compiler_params=pltpu.CompilerParams(
            collective_id=0, has_side_effects=True, vmem_limit_bytes=40 * 1024 * 1024
        ),
        name="adjoint",
    )(*[
        pltpu.with_memory_space_constraint(a, pltpu.HBM)
        for a in (spectral_load, natural_freq, damping, stress_modes, element_volume, row_element, block_case)
    ])
    hbm = pl.BlockSpec(memory_space=pltpu.HBM)
    return pl.pallas_call(
        finish,
        out_shape=(
            jax.ShapeDtypeStruct((2, freq_dev, cases, modes), F32),
            jax.ShapeDtypeStruct((modes,), F32),
        ),
        in_specs=[vmem] * 4,
        out_specs=(hbm, hbm),
        scratch_shapes=[
            pltpu.VMEM((2, freq_dev, cases, modes), F32),
            pltpu.VMEM((modes,), F32),
            dma((9,)),
        ],
        compiler_params=pltpu.CompilerParams(vmem_limit_bytes=16 * 1024 * 1024),
        name="finish",
    )(gq, gd, hr, hi)


def solution(mesh):
    return jax.shard_map(
        per_device,
        mesh=mesh,
        in_specs=(
            P(None, "freq", None, None),
            P(),
            P(),
            P(None, "row"),
            P("row"),
            P("row"),
            P("freq"),
        ),
        out_specs=(P(None, "freq", None, None), P()),
        check_vma=False,
    )
```

```python
import functools
import itertools
import math

import jax
import jax.numpy as jnp
from jax import lax
from jax.experimental import pallas as pl
from jax.experimental.pallas import tpu as pltpu
from jax.sharding import PartitionSpec as P

TBL = 16
MESH = pl.DeviceIdType.MESH
F32 = jnp.float32
BF16 = jnp.bfloat16
SIZES = dict(y=4, zh=4, c=2, zl=4, x=4)


def offsets(*axes):
    steps = itertools.product(*[range(SIZES[a]) for a in axes])
    return [dict(zip(axes, s)) for s in steps if any(s)]


YC = offsets("y", "c")
ZH = offsets("zh")
ZL = offsets("zl")
X = offsets("x")
XY = offsets("x", "y")
XS = [dict(x=d) for d in (1, 3, 2)]
YS = [dict(y=d) for d in (1, 3, 2)]
STEPS = [XS[0], YS[0], XS[1], YS[1], XS[2], YS[2]]
Z = offsets("zh", "zl")
PEERS = ZH + [o for o in Z if o["zl"]] + YC + [o for o in XY if o["x"]]


def cosine(index):
    t = (jnp.abs(index - 1024) - 512).astype(F32) * (math.pi / 1024)
    s = t * t
    poly = -1.0 / 39916800
    for term in (1.0 / 362880, -1.0 / 5040, 1.0 / 120, -1.0 / 6, 1.0):
        poly = poly * s + term
    return t * poly


def kernel(
    lines, scale, load_hbm, nf_hbm, dm_hbm, modes_hbm, ev_hbm, re_hbm, bc_hbm, gq_ref, gd_ref, hr_ref, hi_ref,
    load, nf, dm, stress, ev, re, bc, spec, zspec, usnd, vsnd, urcv, vrcv, own, cbuf, ksnd, kx, kz, kbuf, pu,
    lbuf, dl, gbuf, dbuf, dcore, tab, qr_ref, qi_ref, fwd_ref,
    in_sem, os, orr, c1s, c1r, c2s, c2r, p1s, p1r, v1s, v1r, kxs, kxr, kzs, kzr, kas, kar, kcs, kcr,
    p2s, p2r, ls, lr, dls, dlr, gs, gr, ds, dr, gcs, gcr, dcs, dcr,
):
    fpos = lax.axis_index("freq")
    rpos = lax.axis_index("row")
    me = dict(y=fpos // 8, zh=lax.rem(fpos // 2, 4), c=lax.rem(fpos, 2), zl=rpos // 4, x=lax.rem(rpos, 4))
    y, zh, c, zl, x = me["y"], me["zh"], me["c"], me["zl"], me["x"]
    yc = 2 * y + c
    sent = []

    def at(off):
        return {k: lax.rem(me[k] + off[k], SIZES[k]) if off.get(k) else me[k] for k in SIZES}

    def ident(o):
        return {"freq": o["y"] * 8 + o["zh"] * 2 + o["c"], "row": o["zl"] * 4 + o["x"]}

    def copy_to(src, dst, ssem, rsem, device):
        return pltpu.make_async_remote_copy(
            src_ref=src, dst_ref=dst, send_sem=ssem, recv_sem=rsem, device_id=device, device_id_type=MESH
        )

    def send(src, dst, ssem, rsem, off):
        copy = copy_to(src, dst, ssem, rsem, ident(at(off)))
        copy.start()
        sent.append(copy)
        return copy

    def arrive(copies):
        for copy in copies:
            copy.wait_recv()

    owner = {"freq": zl * 8 + x * 2 + y // 2, "row": rpos}
    orphan = fpos != owner["freq"]
    serves = jnp.logical_and(y == zl, zh == x)
    wards = jnp.where(serves, jnp.where(y // 2 == c, 15, 16), 0)

    barrier = pltpu.get_barrier_semaphore()
    for off in PEERS:
        pl.semaphore_signal(barrier, inc=1, device_id=ident(at(off)), device_id_type=MESH)

    @pl.when(orphan)
    def _():
        pl.semaphore_signal(barrier, inc=1, device_id=owner, device_id_type=MESH)

    modes = nf.shape[0]
    local = [
        pltpu.make_async_copy(src, dst, in_sem.at[i])
        for i, (src, dst) in enumerate([
            (nf_hbm, nf), (dm_hbm, dm), (bc_hbm, bc), (load_hbm, load),
            (re_hbm, re), (ev_hbm, ev), (modes_hbm, stress.at[pl.ds(0, modes)]),
        ])
    ]
    for cp in local:
        cp.start()

    row = lax.broadcasted_iota(jnp.int32, (64, 512), 0)
    lane = lax.broadcasted_iota(jnp.int32, (64, 512), 1)
    ph = jnp.bitwise_and((64 * fpos + (lane % 256) // 4) * (64 * rpos + row) + 512 * (lane // 256), 2047)
    fwd = cosine(ph).reshape(8, 1, 8, 512)
    fwd = jnp.broadcast_to(fwd, (8, 4, 8, 512)).reshape(256, 512)
    row = lax.broadcasted_iota(jnp.int32, (256, 512), 0)
    lane = lax.broadcasted_iota(jnp.int32, (256, 512), 1)
    fwd = jnp.where((row // 8) % 4 == lane % 4, fwd, 0.0).astype(BF16)

    for cp in local[:4]:
        cp.wait()
    row = lax.broadcasted_iota(jnp.int32, (256, modes), 0)
    wf = (2 * (64 * fpos + row // 4) + 1).astype(F32) * (1.0 / lines)
    wm = nf[...].reshape(1, modes)
    wm2 = wm * wm
    den_real = wm2 - wf * wf
    den_imag = 2.0 * dm[...].reshape(1, modes) * wm * wf
    gain = wm2 / (den_real * den_real + den_imag * den_imag)
    h_real = gain * den_real
    h_imag = -gain * den_imag
    hr_ref[...] = h_real
    hi_ref[...] = h_imag
    l_real = load[0].astype(F32).reshape(256, modes)
    l_imag = load[1].astype(F32).reshape(256, modes)
    q_real = l_real * h_real - l_imag * h_imag
    q_imag = l_real * h_imag + l_imag * h_real
    spec[pl.ds(0, 256), :] = q_real.astype(BF16)
    spec[pl.ds(256, 256), :] = q_imag.astype(BF16)
    qr_ref[...] = q_real
    qi_ref[...] = q_imag
    usnd[...] = jnp.dot(fwd, spec[...], preferred_element_type=F32).astype(BF16).reshape(8, 32, modes)
    fwd_ref[...] = fwd
    urcv[yc] = usnd[yc]
    for b in range(2):
        cbuf[zh, yc, pl.ds(b, 1), :] = jnp.full((1, 128), bc[b], jnp.int32).astype(F32)

    for cp in local[4:]:
        cp.wait()
    elem = re[...].reshape(1, re.shape[0]) - rpos * ev.shape[0]
    eye = lax.broadcasted_iota(jnp.int32, (128, 128), 0) == lax.broadcasted_iota(jnp.int32, (128, 128), 1)
    vol = jnp.broadcast_to(ev[...].reshape(1, 128), (128, 128))
    vol = jnp.sum(jnp.where(eye, vol, 0.0), axis=1, keepdims=True)
    onehot = lax.broadcasted_iota(jnp.int32, (128, elem.shape[1]), 0) == elem
    weight = jnp.sum(jnp.where(onehot, vol, 0.0), axis=0, keepdims=True) * (2.0 * scale)
    stress[pl.ds(modes, 768 - modes), :] = jnp.zeros((768 - modes, stress.shape[1]), BF16)
    part = stress[pl.ds(pl.multiple_of(96 * yc, 32), 96), :].astype(F32) * weight
    kpart = lax.dot_general(
        part.astype(BF16), stress[pl.ds(0, modes), :], (((1,), (1,)), ((), ())), preferred_element_type=F32
    )
    ksnd[...] = kpart.reshape(4, 3, 8, modes).astype(BF16)
    kx[x] = ksnd[x]

    pl.semaphore_wait(barrier, len(PEERS) + wards)

    served = []
    for i, (dz, dy, e) in enumerate(itertools.product((2, 1, 3, 0), range(2), range(2))):
        target = (2 * c + dy) * 8 + lax.rem(zh + dz, 4) * 2 + e
        served.append((target, copy_to(cbuf.at[zh, yc], own, os.at[i], orr, {"freq": target, "row": rpos})))

    @pl.when(serves)
    def _():
        for target, cp in served:
            @pl.when(target != fpos)
            def _(cp=cp):
                cp.start()

    p1 = []
    for i, o in enumerate(YC):
        t = at(o)
        p1.append(send(usnd.at[2 * t["y"] + t["c"]], urcv.at[yc], p1s.at[i], p1r.at[i], o))

    kxc = [send(ksnd.at[at(o)["x"]], kx.at[x], kxs.at[i], kxr.at[i], o) for i, o in enumerate(X)]

    row = lax.broadcasted_iota(jnp.int32, (256, modes), 0)
    ratio = (2 * (64 * fpos + row // 4) + 1).astype(F32) * (2.0 / lines) / nf[...].reshape(1, modes)
    zspec[pl.ds(0, 256), :] = (ratio * (qr_ref[...] * hi_ref[...] + qi_ref[...] * hr_ref[...])).astype(BF16)
    zspec[pl.ds(256, 256), :] = (ratio * (qi_ref[...] * hi_ref[...] - qr_ref[...] * hr_ref[...])).astype(BF16)
    vsnd[...] = jnp.dot(fwd_ref[...], zspec[...], preferred_element_type=F32).astype(BF16).reshape(8, 32, modes)
    vrcv[yc] = vsnd[yc]
    v1 = []
    for i, o in enumerate(YC):
        t = at(o)
        v1.append(send(vsnd.at[2 * t["y"] + t["c"]], vrcv.at[yc], v1s.at[i], v1r.at[i], o))
    c1 = [send(cbuf.at[zh, yc], cbuf.at[zh, yc], c1s.at[i], c1r.at[i], o) for i, o in enumerate(YC)]

    arrive(kxc)
    kz[zl] = jnp.sum(kx[...].astype(F32), axis=0).astype(BF16)
    kzc = [send(kz.at[zl], kz.at[zl], kzs.at[i], kzr.at[i], o) for i, o in enumerate(ZL)]
    arrive(c1)
    c2 = [send(cbuf.at[zh], cbuf.at[zh], c2s.at[i], c2r.at[i], o) for i, o in enumerate(ZH)]

    arrive(p1)
    usum = jnp.sum(urcv[...].astype(F32), axis=0)

    @pl.when(orphan)
    def _():
        copy_to(cbuf.at[zh, yc], own, os.at[0], orr, owner).wait_recv()

    @pl.when(jnp.logical_not(orphan))
    def _():
        own[...] = cbuf[zh, yc]

    case = jnp.where(lax.rem(y, 2) == 0, own[0:1, 0:1], own[1:2, 0:1])

    def pick(rows):
        sel = jnp.zeros((8, modes), F32)
        for k in range(4):
            sel = jnp.where(case == k, rows[8 * k:8 * k + 8], sel)
        return sel

    pu[zh] = pick(usum).astype(BF16)
    p2 = [send(pu.at[zh], pu.at[zh], p2s.at[i], p2r.at[i], o) for i, o in enumerate(ZH)]
    arrive(kzc)
    kbuf[y, c, x] = jnp.sum(kz[...].astype(F32), axis=0).astype(BF16)
    kfirst = []
    for i, o in enumerate(STEPS):
        kfirst.append((o, send(kbuf.at[y, c, x], kbuf.at[y, c, x], kas.at[i], kar.at[i], o)))
    ksecond = []
    for o, cp in kfirst:
        arrive([cp])
        piece = kbuf.at[lax.rem(y + 4 - o.get("y", 0), 4), c, lax.rem(x + 4 - o.get("x", 0), 4)]
        piece = piece.at[pl.ds(0, 2)] if "x" in o else piece.at[pl.ds(2, 1)]
        for o2 in YS if "x" in o else XS:
            n = 6 + len(ksecond)
            ksecond.append(send(piece, piece, kas.at[n], kar.at[n], o2))
    arrive(p2)
    factor = float(lines) ** -0.5
    usel = (jnp.sum(pu[...].astype(F32), axis=0) * factor).astype(BF16)
    lbuf[zl] = usel
    lc = [send(lbuf.at[zl], lbuf.at[zl], ls.at[i], lr.at[i], o) for i, o in enumerate(ZL)]
    arrive(ksecond)
    kcc = send(kbuf.at[:, c], kbuf.at[:, c], kcs, kcr, dict(c=1))
    arrive(v1)
    vsel = pick(jnp.sum(vrcv[...].astype(F32), axis=0)) * factor
    arrive([kcc])
    kmat = kbuf[...].reshape(32, 24, modes)[0:25].reshape(600, modes)
    g = jnp.dot(usel, kmat, preferred_element_type=F32).astype(BF16).astype(F32)
    dl[zh, zl] = jnp.sum(g * vsel, axis=0, keepdims=True)
    dlc = [send(dl.at[zh, zl], dl.at[zh, zl], dls.at[i], dlr.at[i], o) for i, o in enumerate(Z)]
    arrive(lc)

    slot = 4 * x + y

    def origin(o):
        return 4 * lax.rem(x + 4 - o.get("x", 0), 4) + lax.rem(y + 4 - o.get("y", 0), 4)

    def sibling(b, i):
        return send(gbuf.at[c, b], gbuf.at[c, b], gcs.at[i], gcr.at[i], dict(c=1))

    gbuf[c, slot] = lbuf[...].astype(F32).reshape(32, modes).astype(BF16)
    first = []
    for i, o in enumerate(STEPS):
        first.append((o, send(gbuf.at[c, slot], gbuf.at[c, slot], gs.at[i], gr.at[i], o)))
    fc = [sibling(slot, 0)]
    second = []
    for o, cp in first:
        arrive([cp])
        b = origin(o)
        half = pl.ds(0 if "x" in o else 16, 16)
        for o2 in YS if "x" in o else XS:
            n = 6 + len(second)
            copy = send(gbuf.at[c, b, half], gbuf.at[c, b, half], gs.at[n], gr.at[n], o2)
            second.append(({**o, **o2}, copy))
        fc.append(sibling(b, len(fc)))

    arrive(c2)
    spread = (
        lax.broadcasted_iota(jnp.int32, (512, 128), 0) // 4 == lax.broadcasted_iota(jnp.int32, (512, 128), 1)
    ).astype(BF16)
    rcase = (lax.broadcasted_iota(jnp.int32, (512, 128), 0) % 4).astype(F32)
    trow = lax.broadcasted_iota(jnp.int32, (128, 128), 0)
    tlane = lax.broadcasted_iota(jnp.int32, (128, 128), 1)
    clane = lax.broadcasted_iota(jnp.int32, (1, 128), 1)
    for xs in range(4):
        cases = jnp.zeros((1, 128), F32)
        for ys in range(4):
            for zs in range(4):
                mine = jnp.logical_and(clane // 32 == ys, (clane // 8) % 4 == zs)
                cases = jnp.where(mine, cbuf[xs, 2 * zs + ys // 2, pl.ds(ys % 2, 1), :], cases)
        keep = rcase == cases
        for cs in range(2):
            n = 64 * (4 * ((tlane // 8) % 4) + xs) + 8 * (2 * (tlane // 32) + cs) + tlane % 8
            ph = jnp.bitwise_and((64 * fpos + trow % 64) * n + 512 * (trow // 64), 2047)
            wide = jnp.dot(spread, cosine(ph).astype(BF16), preferred_element_type=F32)
            tab[cs, :, pl.ds(128 * xs, 128)] = jnp.where(keep, wide, 0.0).astype(BF16)

    arrive(dlc)
    dbuf[slot] = jnp.sum(dl[...], axis=(0, 1))
    dc = [send(dbuf.at[slot], dbuf.at[slot], ds.at[i], dr.at[i], o) for i, o in enumerate(XY)]
    halves = {}
    for o, cp in second:
        arrive([cp])
        key = (o["x"], o["y"])
        halves[key] = halves.get(key, 0) + 1
        if halves[key] == 2:
            fc.append(sibling(origin(o), len(fc)))
    gt = jnp.dot(tab[c], gbuf[c].reshape(512, modes), preferred_element_type=F32)
    arrive(dc)
    dcore[c] = jnp.sum(dbuf[...], axis=0)
    dcc = send(dcore.at[c], dcore.at[c], dcs, dcr, dict(c=1))
    arrive(fc)
    gt += jnp.dot(tab[1 - c], gbuf[1 - c].reshape(512, modes), preferred_element_type=F32)
    gq = jnp.dot(gt.astype(BF16), kmat, preferred_element_type=F32) * factor
    gq_ref[0] = gq[0:256]
    gq_ref[1] = gq[256:512]
    arrive([dcc])
    gd_ref[...] = dcore[0] + dcore[1]

    @pl.when(serves)
    def _():
        for target, cp in served:
            @pl.when(target != fpos)
            def _(cp=cp):
                cp.wait_send()

    for cp in sent:
        cp.wait_send()


def finish(gq, gd, hr, hi, out_hbm, gd_hbm, out, gdv, sems):
    modes = hr.shape[1]
    gdv[...] = gd[...].reshape(modes)
    copies = [pltpu.make_async_copy(gdv, gd_hbm, sems.at[8])]
    copies[0].start()
    for b in range(4):
        rows = pl.ds(64 * b, 64)
        lines = pl.ds(16 * b, 16)
        out[0, lines] = (gq[0, rows, :] * hr[rows, :] + gq[1, rows, :] * hi[rows, :]).reshape(16, 4, modes)
        out[1, lines] = (gq[1, rows, :] * hr[rows, :] - gq[0, rows, :] * hi[rows, :]).reshape(16, 4, modes)
        for k in range(2):
            copy = pltpu.make_async_copy(out.at[k, lines], out_hbm.at[k, lines], sems.at[2 * b + k])
            copy.start()
            copies.append(copy)
    for copy in copies:
        copy.wait()


def per_device(spectral_load, natural_freq, damping, stress_modes, element_volume, row_element, block_case):
    _, freq_dev, cases, modes = spectral_load.shape
    lines = freq_dev * lax.axis_size("freq")
    rows = stress_modes.shape[1]
    times = block_case.shape[0] * TBL * lax.axis_size("freq")
    scale = float(modes * lines) / float(rows * lax.axis_size("row") * times)
    hbm = pl.BlockSpec(memory_space=pltpu.HBM)
    vmem = pl.BlockSpec(memory_space=pltpu.VMEM)
    dma = pltpu.SemaphoreType.DMA
    pairs = [7, 3, 7, 7, 3, 3, 24, None, 3, 3, 15, 24, 15, 16, None]
    gq, gd, hr, hi = pl.pallas_call(
        functools.partial(kernel, lines, scale),
        out_shape=(
            pltpu.VMEM((2, freq_dev * cases, modes), F32),
            pltpu.VMEM((1, modes), F32),
            pltpu.VMEM((freq_dev * cases, modes), F32),
            pltpu.VMEM((freq_dev * cases, modes), F32),
        ),
        in_specs=[hbm] * 7,
        out_specs=(vmem,) * 4,
        scratch_shapes=[
            pltpu.VMEM((2, freq_dev, cases, modes), BF16),
            pltpu.VMEM((modes,), F32),
            pltpu.VMEM((modes,), F32),
            pltpu.VMEM((768, rows), BF16),
            pltpu.VMEM(element_volume.shape, F32),
            pltpu.VMEM(row_element.shape, jnp.int32),
            pltpu.SMEM(block_case.shape, jnp.int32),
            pltpu.VMEM((512, modes), BF16),
            pltpu.VMEM((512, modes), BF16),
            pltpu.VMEM((8, 32, modes), BF16),
            pltpu.VMEM((8, 32, modes), BF16),
            pltpu.VMEM((8, 32, modes), BF16),
            pltpu.VMEM((8, 32, modes), BF16),
            pltpu.VMEM((2, 128), F32),
            pltpu.VMEM((4, 8, 2, 128), F32),
            pltpu.VMEM((4, 3, 8, modes), BF16),
            pltpu.VMEM((4, 3, 8, modes), BF16),
            pltpu.VMEM((4, 3, 8, modes), BF16),
            pltpu.VMEM((4, 2, 4, 3, 8, modes), BF16),
            pltpu.VMEM((4, 8, modes), BF16),
            pltpu.VMEM((4, 8, modes), BF16),
            pltpu.VMEM((4, 4, 1, modes), F32),
            pltpu.VMEM((2, 16, 32, modes), BF16),
            pltpu.VMEM((16, 1, modes), F32),
            pltpu.VMEM((2, 1, modes), F32),
            pltpu.VMEM((2, 512, 512), BF16),
            pltpu.VMEM((256, modes), F32),
            pltpu.VMEM((256, modes), F32),
            pltpu.VMEM((256, 512), BF16),
            dma((7,)), dma((16,)), dma,
        ] + [dma if s is None else dma((s,)) for s in pairs for _ in range(2)],
        compiler_params=pltpu.CompilerParams(
            collective_id=0, has_side_effects=True, vmem_limit_bytes=40 * 1024 * 1024
        ),
        name="adjoint",
    )(*[
        pltpu.with_memory_space_constraint(a, pltpu.HBM)
        for a in (spectral_load, natural_freq, damping, stress_modes, element_volume, row_element, block_case)
    ])
    hbm = pl.BlockSpec(memory_space=pltpu.HBM)
    return pl.pallas_call(
        finish,
        out_shape=(
            jax.ShapeDtypeStruct((2, freq_dev, cases, modes), F32),
            jax.ShapeDtypeStruct((modes,), F32),
        ),
        in_specs=[vmem] * 4,
        out_specs=(hbm, hbm),
        scratch_shapes=[
            pltpu.VMEM((2, freq_dev, cases, modes), F32),
            pltpu.VMEM((modes,), F32),
            dma((9,)),
        ],
        compiler_params=pltpu.CompilerParams(vmem_limit_bytes=16 * 1024 * 1024),
        name="finish",
    )(gq, gd, hr, hi)


def solution(mesh):
    return jax.shard_map(
        per_device,
        mesh=mesh,
        in_specs=(
            P(None, "freq", None, None),
            P(),
            P(),
            P(None, "row"),
            P("row"),
            P("row"),
            P("freq"),
        ),
        out_specs=(P(None, "freq", None, None), P()),
        check_vma=False,
    )
```

```python
import functools
import itertools
import math

import jax
import jax.numpy as jnp
from jax import lax
from jax.experimental import pallas as pl
from jax.experimental.pallas import tpu as pltpu
from jax.sharding import PartitionSpec as P

TBL = 16
MESH = pl.DeviceIdType.MESH
F32 = jnp.float32
BF16 = jnp.bfloat16
SIZES = dict(y=4, zh=4, c=2, zl=4, x=4)


def offsets(*axes):
    steps = itertools.product(*[range(SIZES[a]) for a in axes])
    return [dict(zip(axes, s)) for s in steps if any(s)]


YC = offsets("y", "c")
ZH = offsets("zh")
ZL = offsets("zl")
X = offsets("x")
XY = offsets("x", "y")
XS = [dict(x=d) for d in (1, 3, 2)]
YS = [dict(y=d) for d in (1, 3, 2)]
Z = offsets("zh", "zl")
PEERS = ZH + [o for o in Z if o["zl"]] + YC + [o for o in XY if o["x"]]


def cosine(index):
    t = (jnp.abs(index - 1024) - 512).astype(F32) * (math.pi / 1024)
    s = t * t
    poly = -1.0 / 39916800
    for term in (1.0 / 362880, -1.0 / 5040, 1.0 / 120, -1.0 / 6, 1.0):
        poly = poly * s + term
    return t * poly


def kernel(
    lines, scale, load_hbm, nf_hbm, dm_hbm, modes_hbm, ev_hbm, re_hbm, bc_hbm, gq_ref, gd_ref, hr_ref, hi_ref,
    load, nf, dm, stress, ev, re, bc, spec, zspec, usnd, vsnd, urcv, vrcv, own, cbuf, ksnd, kx, kz, kbuf, pu,
    lbuf, dl, gbuf, dbuf, dcore, tab, qr_ref, qi_ref, fwd_ref,
    in_sem, os, orr, c1s, c1r, c2s, c2r, p1s, p1r, v1s, v1r, kxs, kxr, kzs, kzr, kas, kar, kcs, kcr,
    p2s, p2r, ls, lr, dls, dlr, gs, gr, ds, dr, gcs, gcr, dcs, dcr,
):
    fpos = lax.axis_index("freq")
    rpos = lax.axis_index("row")
    me = dict(y=fpos // 8, zh=lax.rem(fpos // 2, 4), c=lax.rem(fpos, 2), zl=rpos // 4, x=lax.rem(rpos, 4))
    y, zh, c, zl, x = me["y"], me["zh"], me["c"], me["zl"], me["x"]
    yc = 2 * y + c
    sent = []

    def at(off):
        return {k: lax.rem(me[k] + off[k], SIZES[k]) if off.get(k) else me[k] for k in SIZES}

    def ident(o):
        return {"freq": o["y"] * 8 + o["zh"] * 2 + o["c"], "row": o["zl"] * 4 + o["x"]}

    def copy_to(src, dst, ssem, rsem, device):
        return pltpu.make_async_remote_copy(
            src_ref=src, dst_ref=dst, send_sem=ssem, recv_sem=rsem, device_id=device, device_id_type=MESH
        )

    def send(src, dst, ssem, rsem, off):
        copy = copy_to(src, dst, ssem, rsem, ident(at(off)))
        copy.start()
        sent.append(copy)
        return copy

    def arrive(copies):
        for copy in copies:
            copy.wait_recv()

    owner = {"freq": zl * 8 + x * 2 + y // 2, "row": rpos}
    orphan = fpos != owner["freq"]
    serves = jnp.logical_and(y == zl, zh == x)
    wards = jnp.where(serves, jnp.where(y // 2 == c, 15, 16), 0)

    barrier = pltpu.get_barrier_semaphore()
    for off in PEERS:
        pl.semaphore_signal(barrier, inc=1, device_id=ident(at(off)), device_id_type=MESH)

    @pl.when(orphan)
    def _():
        pl.semaphore_signal(barrier, inc=1, device_id=owner, device_id_type=MESH)

    modes = nf.shape[0]
    local = [
        pltpu.make_async_copy(src, dst, in_sem.at[i])
        for i, (src, dst) in enumerate([
            (nf_hbm, nf), (dm_hbm, dm), (bc_hbm, bc), (load_hbm, load),
            (re_hbm, re), (ev_hbm, ev), (modes_hbm, stress.at[pl.ds(0, modes)]),
        ])
    ]
    for cp in local:
        cp.start()

    row = lax.broadcasted_iota(jnp.int32, (64, 512), 0)
    lane = lax.broadcasted_iota(jnp.int32, (64, 512), 1)
    ph = jnp.bitwise_and((64 * fpos + (lane % 256) // 4) * (64 * rpos + row) + 512 * (lane // 256), 2047)
    fwd = cosine(ph).reshape(8, 1, 8, 512)
    fwd = jnp.broadcast_to(fwd, (8, 4, 8, 512)).reshape(256, 512)
    row = lax.broadcasted_iota(jnp.int32, (256, 512), 0)
    lane = lax.broadcasted_iota(jnp.int32, (256, 512), 1)
    fwd = jnp.where((row // 8) % 4 == lane % 4, fwd, 0.0).astype(BF16)

    for cp in local[:4]:
        cp.wait()
    row = lax.broadcasted_iota(jnp.int32, (256, modes), 0)
    wf = (2 * (64 * fpos + row // 4) + 1).astype(F32) * (1.0 / lines)
    wm = nf[...].reshape(1, modes)
    wm2 = wm * wm
    den_real = wm2 - wf * wf
    den_imag = 2.0 * dm[...].reshape(1, modes) * wm * wf
    gain = wm2 / (den_real * den_real + den_imag * den_imag)
    h_real = gain * den_real
    h_imag = -gain * den_imag
    hr_ref[...] = h_real
    hi_ref[...] = h_imag
    l_real = load[0].astype(F32).reshape(256, modes)
    l_imag = load[1].astype(F32).reshape(256, modes)
    q_real = l_real * h_real - l_imag * h_imag
    q_imag = l_real * h_imag + l_imag * h_real
    spec[pl.ds(0, 256), :] = q_real.astype(BF16)
    spec[pl.ds(256, 256), :] = q_imag.astype(BF16)
    qr_ref[...] = q_real
    qi_ref[...] = q_imag
    usnd[...] = jnp.dot(fwd, spec[...], preferred_element_type=F32).astype(BF16).reshape(8, 32, modes)
    fwd_ref[...] = fwd
    urcv[yc] = usnd[yc]
    for b in range(2):
        cbuf[zh, yc, pl.ds(b, 1), :] = jnp.full((1, 128), bc[b], jnp.int32).astype(F32)


    pl.semaphore_wait(barrier, len(PEERS) + wards)

    served = []
    for i, (dz, dy, e) in enumerate(itertools.product((2, 1, 3, 0), range(2), range(2))):
        target = (2 * c + dy) * 8 + lax.rem(zh + dz, 4) * 2 + e
        served.append((target, copy_to(cbuf.at[zh, yc], own, os.at[i], orr, {"freq": target, "row": rpos})))

    @pl.when(serves)
    def _():
        for target, cp in served:
            @pl.when(target != fpos)
            def _(cp=cp):
                cp.start()

    p1 = []
    for i, o in enumerate(YC):
        t = at(o)
        p1.append(send(usnd.at[2 * t["y"] + t["c"]], urcv.at[yc], p1s.at[i], p1r.at[i], o))

    for cp in local[4:]:
        cp.wait()
    elem = re[...].reshape(1, re.shape[0]) - rpos * ev.shape[0]
    eye = lax.broadcasted_iota(jnp.int32, (128, 128), 0) == lax.broadcasted_iota(jnp.int32, (128, 128), 1)
    vol = jnp.broadcast_to(ev[...].reshape(1, 128), (128, 128))
    vol = jnp.sum(jnp.where(eye, vol, 0.0), axis=1, keepdims=True)
    onehot = lax.broadcasted_iota(jnp.int32, (128, elem.shape[1]), 0) == elem
    weight = jnp.sum(jnp.where(onehot, vol, 0.0), axis=0, keepdims=True) * (2.0 * scale)
    stress[pl.ds(modes, 768 - modes), :] = jnp.zeros((768 - modes, stress.shape[1]), BF16)
    part = stress[pl.ds(pl.multiple_of(96 * yc, 32), 96), :].astype(F32) * weight
    kpart = lax.dot_general(
        part.astype(BF16), stress[pl.ds(0, modes), :], (((1,), (1,)), ((), ())), preferred_element_type=F32
    )
    ksnd[...] = kpart.reshape(4, 3, 8, modes).astype(BF16)
    kx[x] = ksnd[x]
    kxc = [send(ksnd.at[at(o)["x"]], kx.at[x], kxs.at[i], kxr.at[i], o) for i, o in enumerate(X)]

    row = lax.broadcasted_iota(jnp.int32, (256, modes), 0)
    ratio = (2 * (64 * fpos + row // 4) + 1).astype(F32) * (2.0 / lines) / nf[...].reshape(1, modes)
    zspec[pl.ds(0, 256), :] = (ratio * (qr_ref[...] * hi_ref[...] + qi_ref[...] * hr_ref[...])).astype(BF16)
    zspec[pl.ds(256, 256), :] = (ratio * (qi_ref[...] * hi_ref[...] - qr_ref[...] * hr_ref[...])).astype(BF16)
    vsnd[...] = jnp.dot(fwd_ref[...], zspec[...], preferred_element_type=F32).astype(BF16).reshape(8, 32, modes)
    vrcv[yc] = vsnd[yc]
    v1 = []
    for i, o in enumerate(YC):
        t = at(o)
        v1.append(send(vsnd.at[2 * t["y"] + t["c"]], vrcv.at[yc], v1s.at[i], v1r.at[i], o))
    c1 = [send(cbuf.at[zh, yc], cbuf.at[zh, yc], c1s.at[i], c1r.at[i], o) for i, o in enumerate(YC)]

    arrive(kxc)
    kz[zl] = jnp.sum(kx[...].astype(F32), axis=0).astype(BF16)
    kzc = [send(kz.at[zl], kz.at[zl], kzs.at[i], kzr.at[i], o) for i, o in enumerate(ZL)]

    arrive(p1)
    usum = jnp.sum(urcv[...].astype(F32), axis=0)

    @pl.when(orphan)
    def _():
        copy_to(cbuf.at[zh, yc], own, os.at[0], orr, owner).wait_recv()

    @pl.when(jnp.logical_not(orphan))
    def _():
        own[...] = cbuf[zh, yc]

    case = jnp.where(lax.rem(y, 2) == 0, own[0:1, 0:1], own[1:2, 0:1])

    def pick(rows):
        sel = jnp.zeros((8, modes), F32)
        for k in range(4):
            sel = jnp.where(case == k, rows[8 * k:8 * k + 8], sel)
        return sel

    pu[zh] = pick(usum).astype(BF16)
    p2 = [send(pu.at[zh], pu.at[zh], p2s.at[i], p2r.at[i], o) for i, o in enumerate(ZH)]
    arrive(kzc)
    kbuf[y, c, x] = jnp.sum(kz[...].astype(F32), axis=0).astype(BF16)
    kac = [send(kbuf.at[y, c, x], kbuf.at[y, c, x], kas.at[i], kar.at[i], o) for i, o in enumerate(XY)]
    arrive(p2)
    factor = float(lines) ** -0.5
    usel = (jnp.sum(pu[...].astype(F32), axis=0) * factor).astype(BF16)
    lbuf[zl] = usel
    lc = [send(lbuf.at[zl], lbuf.at[zl], ls.at[i], lr.at[i], o) for i, o in enumerate(ZL)]
    arrive(c1)
    c2 = [send(cbuf.at[zh], cbuf.at[zh], c2s.at[i], c2r.at[i], o) for i, o in enumerate(ZH)]
    arrive(kac)
    kcc = send(kbuf.at[:, c], kbuf.at[:, c], kcs, kcr, dict(c=1))
    arrive(v1)
    vsel = pick(jnp.sum(vrcv[...].astype(F32), axis=0)) * factor
    arrive(lc)

    slot = 4 * x + y

    def origin(o):
        return 4 * lax.rem(x + 4 - o.get("x", 0), 4) + lax.rem(y + 4 - o.get("y", 0), 4)

    def sibling(b, i):
        return send(gbuf.at[c, b], gbuf.at[c, b], gcs.at[i], gcr.at[i], dict(c=1))

    gbuf[c, slot] = lbuf[...].astype(F32).reshape(32, modes).astype(BF16)
    first = []
    for i, o in enumerate([XS[0], YS[0], XS[1], YS[1], XS[2], YS[2]]):
        first.append((o, send(gbuf.at[c, slot], gbuf.at[c, slot], gs.at[i], gr.at[i], o)))
    fc = [sibling(slot, 0)]
    arrive([kcc])
    kmat = kbuf[...].reshape(32, 24, modes)[0:25].reshape(600, modes)
    g = jnp.dot(usel, kmat, preferred_element_type=F32).astype(BF16).astype(F32)
    dl[zh, zl] = jnp.sum(g * vsel, axis=0, keepdims=True)
    dlc = [send(dl.at[zh, zl], dl.at[zh, zl], dls.at[i], dlr.at[i], o) for i, o in enumerate(Z)]
    second = []
    for o, cp in first:
        arrive([cp])
        b = origin(o)
        half = pl.ds(0 if "x" in o else 16, 16)
        for o2 in YS if "x" in o else XS:
            n = 6 + len(second)
            copy = send(gbuf.at[c, b, half], gbuf.at[c, b, half], gs.at[n], gr.at[n], o2)
            second.append(({**o, **o2}, copy))
        fc.append(sibling(b, len(fc)))

    arrive(c2)
    spread = (
        lax.broadcasted_iota(jnp.int32, (512, 128), 0) // 4 == lax.broadcasted_iota(jnp.int32, (512, 128), 1)
    ).astype(BF16)
    rcase = (lax.broadcasted_iota(jnp.int32, (512, 128), 0) % 4).astype(F32)
    trow = lax.broadcasted_iota(jnp.int32, (128, 128), 0)
    tlane = lax.broadcasted_iota(jnp.int32, (128, 128), 1)
    clane = lax.broadcasted_iota(jnp.int32, (1, 128), 1)
    for xs in range(4):
        cases = jnp.zeros((1, 128), F32)
        for ys in range(4):
            for zs in range(4):
                mine = jnp.logical_and(clane // 32 == ys, (clane // 8) % 4 == zs)
                cases = jnp.where(mine, cbuf[xs, 2 * zs + ys // 2, pl.ds(ys % 2, 1), :], cases)
        keep = rcase == cases
        for cs in range(2):
            n = 64 * (4 * ((tlane // 8) % 4) + xs) + 8 * (2 * (tlane // 32) + cs) + tlane % 8
            ph = jnp.bitwise_and((64 * fpos + trow % 64) * n + 512 * (trow // 64), 2047)
            wide = jnp.dot(spread, cosine(ph).astype(BF16), preferred_element_type=F32)
            tab[cs, :, pl.ds(128 * xs, 128)] = jnp.where(keep, wide, 0.0).astype(BF16)

    arrive(dlc)
    dbuf[slot] = jnp.sum(dl[...], axis=(0, 1))
    dc = [send(dbuf.at[slot], dbuf.at[slot], ds.at[i], dr.at[i], o) for i, o in enumerate(XY)]
    halves = {}
    for o, cp in second:
        arrive([cp])
        key = (o["x"], o["y"])
        halves[key] = halves.get(key, 0) + 1
        if halves[key] == 2:
            fc.append(sibling(origin(o), len(fc)))
    gt = jnp.dot(tab[c], gbuf[c].reshape(512, modes), preferred_element_type=F32)
    arrive(dc)
    dcore[c] = jnp.sum(dbuf[...], axis=0)
    dcc = send(dcore.at[c], dcore.at[c], dcs, dcr, dict(c=1))
    arrive(fc)
    gt += jnp.dot(tab[1 - c], gbuf[1 - c].reshape(512, modes), preferred_element_type=F32)
    gq = jnp.dot(gt.astype(BF16), kmat, preferred_element_type=F32) * factor
    gq_ref[0] = gq[0:256]
    gq_ref[1] = gq[256:512]
    arrive([dcc])
    gd_ref[...] = dcore[0] + dcore[1]

    @pl.when(serves)
    def _():
        for target, cp in served:
            @pl.when(target != fpos)
            def _(cp=cp):
                cp.wait_send()

    for cp in sent:
        cp.wait_send()


def finish(gq, gd, hr, hi, out_hbm, gd_hbm, out, gdv, sems):
    modes = hr.shape[1]
    gdv[...] = gd[...].reshape(modes)
    copies = [pltpu.make_async_copy(gdv, gd_hbm, sems.at[8])]
    copies[0].start()
    for b in range(4):
        rows = pl.ds(64 * b, 64)
        lines = pl.ds(16 * b, 16)
        out[0, lines] = (gq[0, rows, :] * hr[rows, :] + gq[1, rows, :] * hi[rows, :]).reshape(16, 4, modes)
        out[1, lines] = (gq[1, rows, :] * hr[rows, :] - gq[0, rows, :] * hi[rows, :]).reshape(16, 4, modes)
        for k in range(2):
            copy = pltpu.make_async_copy(out.at[k, lines], out_hbm.at[k, lines], sems.at[2 * b + k])
            copy.start()
            copies.append(copy)
    for copy in copies:
        copy.wait()


def per_device(spectral_load, natural_freq, damping, stress_modes, element_volume, row_element, block_case):
    _, freq_dev, cases, modes = spectral_load.shape
    lines = freq_dev * lax.axis_size("freq")
    rows = stress_modes.shape[1]
    times = block_case.shape[0] * TBL * lax.axis_size("freq")
    scale = float(modes * lines) / float(rows * lax.axis_size("row") * times)
    hbm = pl.BlockSpec(memory_space=pltpu.HBM)
    vmem = pl.BlockSpec(memory_space=pltpu.VMEM)
    dma = pltpu.SemaphoreType.DMA
    pairs = [7, 3, 7, 7, 3, 3, 15, None, 3, 3, 15, 24, 15, 16, None]
    gq, gd, hr, hi = pl.pallas_call(
        functools.partial(kernel, lines, scale),
        out_shape=(
            pltpu.VMEM((2, freq_dev * cases, modes), F32),
            pltpu.VMEM((1, modes), F32),
            pltpu.VMEM((freq_dev * cases, modes), F32),
            pltpu.VMEM((freq_dev * cases, modes), F32),
        ),
        in_specs=[hbm] * 7,
        out_specs=(vmem,) * 4,
        scratch_shapes=[
            pltpu.VMEM((2, freq_dev, cases, modes), BF16),
            pltpu.VMEM((modes,), F32),
            pltpu.VMEM((modes,), F32),
            pltpu.VMEM((768, rows), BF16),
            pltpu.VMEM(element_volume.shape, F32),
            pltpu.VMEM(row_element.shape, jnp.int32),
            pltpu.SMEM(block_case.shape, jnp.int32),
            pltpu.VMEM((512, modes), BF16),
            pltpu.VMEM((512, modes), BF16),
            pltpu.VMEM((8, 32, modes), BF16),
            pltpu.VMEM((8, 32, modes), BF16),
            pltpu.VMEM((8, 32, modes), BF16),
            pltpu.VMEM((8, 32, modes), BF16),
            pltpu.VMEM((2, 128), F32),
            pltpu.VMEM((4, 8, 2, 128), F32),
            pltpu.VMEM((4, 3, 8, modes), BF16),
            pltpu.VMEM((4, 3, 8, modes), BF16),
            pltpu.VMEM((4, 3, 8, modes), BF16),
            pltpu.VMEM((4, 2, 4, 3, 8, modes), BF16),
            pltpu.VMEM((4, 8, modes), BF16),
            pltpu.VMEM((4, 8, modes), BF16),
            pltpu.VMEM((4, 4, 1, modes), F32),
            pltpu.VMEM((2, 16, 32, modes), BF16),
            pltpu.VMEM((16, 1, modes), F32),
            pltpu.VMEM((2, 1, modes), F32),
            pltpu.VMEM((2, 512, 512), BF16),
            pltpu.VMEM((256, modes), F32),
            pltpu.VMEM((256, modes), F32),
            pltpu.VMEM((256, 512), BF16),
            dma((7,)), dma((16,)), dma,
        ] + [dma if s is None else dma((s,)) for s in pairs for _ in range(2)],
        compiler_params=pltpu.CompilerParams(
            collective_id=0, has_side_effects=True, vmem_limit_bytes=40 * 1024 * 1024
        ),
        name="adjoint",
    )(*[
        pltpu.with_memory_space_constraint(a, pltpu.HBM)
        for a in (spectral_load, natural_freq, damping, stress_modes, element_volume, row_element, block_case)
    ])
    hbm = pl.BlockSpec(memory_space=pltpu.HBM)
    return pl.pallas_call(
        finish,
        out_shape=(
            jax.ShapeDtypeStruct((2, freq_dev, cases, modes), F32),
            jax.ShapeDtypeStruct((modes,), F32),
        ),
        in_specs=[vmem] * 4,
        out_specs=(hbm, hbm),
        scratch_shapes=[
            pltpu.VMEM((2, freq_dev, cases, modes), F32),
            pltpu.VMEM((modes,), F32),
            dma((9,)),
        ],
        compiler_params=pltpu.CompilerParams(vmem_limit_bytes=16 * 1024 * 1024),
        name="finish",
    )(gq, gd, hr, hi)


def solution(mesh):
    return jax.shard_map(
        per_device,
        mesh=mesh,
        in_specs=(
            P(None, "freq", None, None),
            P(),
            P(),
            P(None, "row"),
            P("row"),
            P("row"),
            P("freq"),
        ),
        out_specs=(P(None, "freq", None, None), P()),
        check_vma=False,
    )
```
